32 devices in a mesh: seq: 16 (over z, y, core), head: 2 (over x).
Axes of the slice: x: 2, y: 2, z: 4, core: 2. Of those that a mesh axis runs over, the one named last changes fastest.
Arguments:
- query: bfloat16 [16384, 1024], P('seq', 'head'), may hold values from -48 to 48
- key: bfloat16 [16384, 1024], P('seq', 'head'), may hold values from -48 to 48
- value: bfloat16 [16384, 1024], P('seq', 'head'), may hold values from -6 to 6
- out_grad: bfloat16 [16384, 1024], P('seq', 'head'), may hold values from -6 to 6
- pool_group: float32 [16, 64], P('head'), may hold values from -0.75 to 0.75
- pool_global: float32 [16, 256], P('head'), may hold values from -0.375 to 0.375
Outputs:
- query_grad: bfloat16 [16384, 1024], P('seq', 'head')
- key_grad: bfloat16 [16384, 1024], P('seq', 'head')
- value_grad: bfloat16 [16384, 1024], P('seq', 'head')
The draws below stay inside these ranges and needn't reach their ends.
All inputs are finite; a program needn't handle non-finite values.
Results may differ from the reference program's by a relative error of at most 0.04.
Values may be sent and summed in bfloat16 or wider, within the bound.
No kernel may reach another device: no remote copies, remote signals or barrier semaphores. Data moves between devices by JAX's collectives and lax.ppermute only.
A program may use at most 64 MiB of HBM per device.

```python
import math
import jax
import jax.numpy as jnp
from jax import lax

HEADS = 16
HD = 64
BLOCK = 256
SEG1 = 64
SEG2 = 256
GROUP = 8
TOK_DEV = 1024
TOKENS = 16384


def paired_fields(key):
    base = jax.random.fold_in(key, 31)
    streams = jax.random.split(base, 2)
    shape = (TOKENS, HEADS, HD)
    query_field = jnp.clip(jax.random.normal(streams[0], shape, jnp.float32), -4.0, 4.0)
    key_field = jnp.clip(jax.random.normal(streams[1], shape, jnp.float32), -4.0, 4.0)
    return (query_field, key_field)


def draw_query(key, part):
    return paired_fields(key)[0].reshape(TOKENS, HEADS * HD).astype(jnp.bfloat16)


def draw_key(key, part):
    return paired_fields(key)[1].reshape(TOKENS, HEADS * HD).astype(jnp.bfloat16)


def block_scale(stream_key, shape, shards, smallest, top_value):
    factor_of = 1.0
    for position, shards_of in shards:
        steps = jax.random.uniform(jax.random.fold_in(jax.random.fold_in(stream_key, 6), position), (shards_of,), jnp.float32, smallest / len(shards), top_value / len(shards))
        factor_of = factor_of * jnp.repeat(jnp.exp(steps), shape[position] // shards_of).reshape((-1,) + (1,) * (len(shape) - 1 - position))
    return factor_of


def centred(key, extent, scale, most, cuts=(), kind=jnp.bfloat16):
    level = block_scale(key, extent, cuts, -0.22, 0.18) if cuts else 1.0
    array = jax.random.normal(key, extent, jnp.float32) * scale * level
    return jnp.minimum(jnp.maximum(array, -most), most).astype(kind)


def setup_inputs(seed: int = 0) -> dict:
    splits = jax.random.split(jax.random.key(seed), 7)
    query = draw_query(jax.random.fold_in(splits[6], 71), 0)
    key = draw_key(jax.random.fold_in(splits[6], 71), 0)
    value = centred(splits[2], (TOKENS, HEADS * HD), 1.0, 6.0, ((0, 16), (1, 2)))
    out_grad = centred(splits[3], (TOKENS, HEADS * HD), 1.0, 6.0, ((0, 16), (1, 2)))
    pool_group = centred(splits[4], (HEADS, SEG1), SEG1 ** -0.5, 0.75, ((0, 2),), jnp.float32)
    pool_global = centred(splits[5], (HEADS, SEG2), SEG2 ** -0.5, 0.375, ((0, 2),), jnp.float32)
    return dict(query=query, key=key, value=value, out_grad=out_grad, pool_group=pool_group, pool_global=pool_global)


def pooled(stacked, pool, segment):
    count = stacked.shape[1] // segment
    shaped = stacked.astype(jnp.float32).reshape(2, count, segment, stacked.shape[2], stacked.shape[3])
    return jnp.einsum('nsphd,hp->nshd', shaped, pool.astype(jnp.float32)).astype(jnp.bfloat16)

def spread(grads, pool, segment):
    count = grads.shape[1]
    widened = jnp.einsum('nshd,hp->nsphd', grads, pool.astype(jnp.float32))
    return widened.reshape(2, count * segment, grads.shape[2], grads.shape[3])

def reference(query, key, value, out_grad, pool_group, pool_global):
    scale = 1.0 / math.sqrt(HD)
    queries = query.reshape(TOKENS, HEADS, HD)
    cotangent = out_grad.reshape(TOKENS, HEADS, HD)
    stacked = jnp.stack([key.reshape(TOKENS, HEADS, HD), value.reshape(TOKENS, HEADS, HD)])
    level_one = pooled(stacked, pool_group, SEG1)
    level_two = pooled(stacked, pool_global, SEG2)
    padded = jnp.pad(stacked, ((0, 0), (BLOCK, BLOCK), (0, 0), (0, 0)))
    per_group = GROUP * TOK_DEV // SEG1
    block_count = TOKENS // BLOCK
    window_len = 3 * BLOCK
    offsets = jnp.arange(window_len, dtype=jnp.int32) // BLOCK - 1
    far_len = per_group + level_two.shape[1]

    def step(carry, block_index):
        extended, grads_one, grads_two = carry
        offset = block_index * BLOCK
        query_rows = lax.dynamic_slice_in_dim(queries, offset, BLOCK, 0).astype(jnp.float32)
        grad_rows = lax.dynamic_slice_in_dim(cotangent, offset, BLOCK, 0).astype(jnp.float32)
        window = lax.dynamic_slice_in_dim(padded, offset, window_len, 1)
        group_start = offset // (GROUP * TOK_DEV) * per_group
        own_group = lax.dynamic_slice_in_dim(level_one, group_start, per_group, 1)
        keyset = jnp.concatenate([window, own_group, level_two], axis=1).astype(jnp.float32)
        scores = jnp.einsum('qhd,khd->hqk', query_rows, keyset[0]) * scale
        key_block = block_index + offsets
        inside = (key_block >= 0) & (key_block < block_count)
        inside = jnp.concatenate([inside, jnp.ones((far_len,), dtype=bool)])
        scores = jnp.where(inside, scores, -1e+30)
        highest = lax.optimization_barrier(jnp.max(scores, axis=-1, keepdims=True))
        expon = jnp.exp(scores - highest)
        probs = expon / lax.optimization_barrier(jnp.sum(expon, axis=-1, keepdims=True))
        weights = probs.astype(jnp.bfloat16).astype(jnp.float32)
        attended = jnp.einsum('hqk,khd->qhd', weights, keyset[1])
        delta = lax.optimization_barrier(jnp.sum(grad_rows * attended, axis=-1))
        dprob = jnp.einsum('qhd,khd->hqk', grad_rows, keyset[1])
        dscore = (probs * (dprob - delta.T[:, :, None])).astype(jnp.bfloat16).astype(jnp.float32)
        query_part = (jnp.einsum('hqk,khd->qhd', dscore, keyset[0]) * scale).astype(jnp.bfloat16)
        key_part = jnp.einsum('hqk,qhd->khd', dscore, query_rows) * scale
        value_part = jnp.einsum('hqk,qhd->khd', weights, grad_rows)
        direct = jnp.stack([key_part, value_part])
        current = lax.dynamic_slice_in_dim(extended, offset, window_len, 1)
        extended = lax.dynamic_update_slice_in_dim(extended, current + direct[:, :window_len], offset, 1)
        current_one = lax.dynamic_slice_in_dim(grads_one, group_start, per_group, 1)
        grads_one = lax.dynamic_update_slice_in_dim(grads_one, current_one + direct[:, window_len:window_len + per_group], group_start, 1)
        grads_two = grads_two + direct[:, window_len + per_group:]
        return ((extended, grads_one, grads_two), query_part)
    initial = (jnp.zeros((2, TOKENS + 2 * BLOCK, HEADS, HD), jnp.float32), jnp.zeros((2, TOKENS // SEG1, HEADS, HD), jnp.float32), jnp.zeros((2, TOKENS // SEG2, HEADS, HD), jnp.float32))
    (extended, grads_one, grads_two), query_parts = lax.scan(step, initial, jnp.arange(block_count, dtype=jnp.int32))
    summed = extended[:, BLOCK:BLOCK + TOKENS] + spread(grads_one, pool_group, SEG1) + spread(grads_two, pool_global, SEG2)
    query_grad = query_parts.reshape(TOKENS, HEADS * HD)
    key_grad = summed[0].astype(jnp.bfloat16).reshape(TOKENS, HEADS * HD)
    value_grad = summed[1].astype(jnp.bfloat16).reshape(TOKENS, HEADS * HD)
    return (query_grad, key_grad, value_grad)
```

```python
import functools
import math

import jax
import jax.numpy as jnp
from jax import lax
from jax.experimental import pallas as pl
from jax.experimental.pallas import tpu as pltpu
from jax.sharding import PartitionSpec as P

BLOCK = 256
SEG1 = 64
SEG2 = 256
GROUP = 8
NEG = -1e30
F32 = jnp.float32
BF16 = jnp.bfloat16
NT = (((1,), (1,)), ((), ()))
NN = (((1,), (0,)), ((), ()))
VMEM_LIMIT = 48 * 2**20


def dot(a, b, dims):
    return lax.dot_general(a, b, dims, preferred_element_type=F32)


def struct(shape, dtype):
    return jax.ShapeDtypeStruct(shape, dtype)


def call(body, name, flops=0, moved=0, **kwargs):
    cost = pl.CostEstimate(flops=int(flops), bytes_accessed=int(moved), transcendentals=0)
    params = pltpu.CompilerParams(vmem_limit_bytes=VMEM_LIMIT)
    return pl.pallas_call(body, name=name, cost_estimate=cost, compiler_params=params, **kwargs)


def head_masks(width, depth):
    lane = lax.broadcasted_iota(jnp.int32, (1, width), 1)
    return [(lane >= h * depth) & (lane < (h + 1) * depth) for h in range(width // depth)]


def keep_head(rows, mask, scale=None):
    rows = jnp.where(mask, rows, 0)
    if scale is not None:
        rows = rows.astype(F32) * scale
    return rows.astype(BF16)


def near(block, blocks):
    return range(max(block - 1, 0), min(block + 2, blocks))


def pool_body(k, v, group_pool, whole_pool, own, first, last, wide_group, wide_whole):
    rows, cols = k.shape
    heads = group_pool.shape[0]
    depth = cols // heads
    head = lax.broadcasted_iota(jnp.int32, (heads, cols), 0)
    col = lax.broadcasted_iota(jnp.int32, (heads, cols), 1)
    pick = ((col >= head * depth) & (col < (head + 1) * depth)).astype(F32)
    tn = (((0,), (0,)), ((), ()))
    exact = lax.Precision.HIGHEST
    wide_group[...] = lax.dot_general(
        group_pool[...], pick, tn, precision=exact, preferred_element_type=F32
    )
    wide_whole[...] = lax.dot_general(
        whole_pool[...], pick, tn, precision=exact, preferred_element_type=F32
    )
    count1 = rows // SEG1
    for n, src in enumerate((k, v)):
        first[n] = src[:BLOCK]
        last[n] = src[rows - BLOCK :]
        sums = []
        for s in range(count1):
            part = src[s * SEG1 : (s + 1) * SEG1].astype(F32) * wide_group[...]
            sums.append(jnp.sum(part, axis=0, keepdims=True))
        for s in range(rows // SEG2):
            part = src[s * SEG2 : (s + 1) * SEG2].astype(F32) * wide_whole[...]
            sums.append(jnp.sum(part, axis=0, keepdims=True))
        pad = own.shape[2] - len(sums)
        if pad:
            sums.append(jnp.zeros((pad, cols), F32))
        own[0, n] = jnp.concatenate(sums, axis=0).astype(BF16)


def pool(k, v, group_pool, whole_pool):
    rows, cols = k.shape
    count = rows // SEG1 + rows // SEG2
    padded = -(-count // 8) * 8
    return call(
        pool_body,
        "pool",
        moved=k.size * 8,
        out_shape=[
            struct((1, 2, padded, cols), BF16),
            struct((2, BLOCK, cols), BF16),
            struct((2, BLOCK, cols), BF16),
            struct((SEG1, cols), F32),
            struct((SEG2, cols), F32),
        ],
    )(k, v, group_pool, whole_pool)


def pack_body(count1, count2, comb, whole, out):
    slots1, slots2 = comb.shape[0], whole.shape[0]
    for n in range(2):
        parts = [comb[s, n, :count1] for s in range(slots1)]
        parts += [whole[s, n] for s in range(slots2)]
        out[n] = jnp.concatenate([p.astype(F32) for p in parts], axis=0).astype(BF16)


def pack(comb, whole, count1, count2):
    cols = comb.shape[-1]
    rows = comb.shape[0] * count1 + whole.shape[0] * count2
    return call(
        functools.partial(pack_body, count1, count2),
        "pack",
        moved=comb.size * 4,
        out_shape=struct((2, rows, cols), BF16),
    )(comb, whole)


def stats_body(depth, scale, q, k, v, g, out):
    rows, width = q.shape
    blocks = rows // BLOCK
    chunk = 64
    for h, mask in enumerate(head_masks(width, depth)):
        for b in range(blocks):
            r = slice(b * BLOCK, (b + 1) * BLOCK)
            qs = keep_head(q[r], mask, scale)
            gs = keep_head(g[r], mask)
            lo, hi = near(b, blocks)[0] * BLOCK, (near(b, blocks)[-1] + 1) * BLOCK
            s_all = dot(k[lo:hi], qs, NT)
            d_all = dot(v[lo:hi], gs, NT)
            top = total = inner = None
            for c in range(0, hi - lo, chunk):
                s = s_all[c : c + chunk].reshape(chunk // 8, 8, BLOCK)
                d = d_all[c : c + chunk].reshape(chunk // 8, 8, BLOCK)
                here = jnp.max(s, axis=0)
                if top is None:
                    new = here
                else:
                    new = jnp.maximum(top, here)
                e = jnp.exp(s - new[None])
                sum_e = jnp.sum(e, axis=0)
                sum_d = jnp.sum(e * d, axis=0)
                if top is not None:
                    fade = jnp.exp(top - new)
                    sum_e = sum_e + total * fade
                    sum_d = sum_d + inner * fade
                top, total, inner = new, sum_e, sum_d
            most = jnp.max(top, axis=0, keepdims=True)
            fade = jnp.exp(top - most)
            out[0, h : h + 1, r] = most
            out[1, h : h + 1, r] = jnp.sum(total * fade, axis=0, keepdims=True)
            out[2, h : h + 1, r] = jnp.sum(inner * fade, axis=0, keepdims=True)


def stats(q, k, v, g, width, depth, scale, pair):
    rows = q.shape[0]
    hp = width // depth
    cols = pl.BlockSpec((rows, width), lambda i: (0, pair))
    return call(
        functools.partial(stats_body, depth, scale),
        f"stats{pair}",
        flops=2 * 2 * 3 * BLOCK * rows * width,
        moved=rows * width * 8,
        grid=(1,),
        in_specs=[cols] * 4,
        out_specs=pl.BlockSpec((3, hp, rows), lambda i: (0, 0, 0)),
        out_shape=struct((3, hp, rows), F32),
    )(q, k, v, g)


def remote_body(
    depth, scale, pairs, ends, q, g, before, after, mine, theirs, *rest
):
    partial = rest[:pairs]
    kept, sent, to_prev, to_next, dq_t, final, far_k, far_v = rest[pairs : pairs + 8]
    far_kt, near_t, q_t, g_t, dk_t, dv_t = rest[pairs + 8 :]
    rows, width = q.shape
    blocks = rows // BLOCK
    half = mine.shape[1]
    far = 2 * half
    pair = pl.program_id(0)
    far_k[:half] = mine[0]
    far_k[half:] = theirs[0]
    far_v[:half] = mine[1]
    far_v[half:] = theirs[1]
    far_kt[...] = (far_k[...].astype(F32) * scale).astype(BF16).T
    near_t[0] = (before[0].astype(F32) * scale).astype(BF16).T
    near_t[1] = (after[0].astype(F32) * scale).astype(BF16).T
    q_t[...] = (q[...].astype(F32) * scale).astype(BF16).T
    g_t[...] = g[...].T
    low = jnp.where(ends[0] == 1, NEG, 0.0)
    high = jnp.where(ends[1] == 1, NEG, 0.0)
    for h, mask in enumerate(head_masks(width, depth)):
        hr = slice(h * depth, (h + 1) * depth)
        for b in range(blocks):
            r = slice(b * BLOCK, (b + 1) * BLOCK)
            qs = keep_head(q[r], mask, scale)
            gs = keep_head(g[r], mask)
            scores = [dot(far_k[...], qs, NT)]
            values = [dot(far_v[...], gs, NT)]
            if b == 0:
                scores.append(dot(before[0], qs, NT) + low)
                values.append(dot(before[1], gs, NT))
            if b == blocks - 1:
                scores.append(dot(after[0], qs, NT) + high)
                values.append(dot(after[1], gs, NT))
            old = [partial[0][n, h : h + 1, r] for n in range(3)]
            for n in range(1, pairs):
                old = [
                    jnp.where(pair == n, partial[n][m, h : h + 1, r], old[m]) for m in range(3)
                ]
            top = old[0]
            for s in scores:
                top = jnp.maximum(top, jnp.max(s, axis=0, keepdims=True))
            fade = jnp.exp(old[0] - top)
            total = old[1] * fade
            inner = old[2] * fade
            exps = []
            for s, d in zip(scores, values):
                e = jnp.exp(s - top)
                exps.append(e)
                total = total + jnp.sum(e, axis=0, keepdims=True)
                inner = inner + jnp.sum(e * d, axis=0, keepdims=True)
            share = 1.0 / total
            delta = inner * share
            final[0, h : h + 1, r] = top + jnp.log(total)
            final[1, h : h + 1, r] = delta
            probs = [e * share for e in exps]
            grads = [(p * (d - delta)).astype(BF16) for p, d in zip(probs, values)]
            weights = [p.astype(BF16) for p in probs]
            qt, gt = q_t[hr, r], g_t[hr, r]
            dv = dot(gt, weights[0], NT)
            dk = dot(qt, grads[0], NT)
            if b == 0:
                dv_t[hr, :far] = dv
                dk_t[hr, :far] = dk
            else:
                dv_t[hr, :far] += dv
                dk_t[hr, :far] += dk
            dq = dot(far_kt[hr], grads[0], NN)
            at = 1
            if b == 0:
                dv_t[hr, far : far + BLOCK] = dot(gt, weights[at], NT)
                dk_t[hr, far : far + BLOCK] = dot(qt, grads[at], NT)
                dq = dq + dot(near_t[0, hr], grads[at], NN)
                at += 1
            if b == blocks - 1:
                dv_t[hr, far + BLOCK :] = dot(gt, weights[at], NT)
                dk_t[hr, far + BLOCK :] = dot(qt, grads[at], NT)
                dq = dq + dot(near_t[1, hr], grads[at], NN)
            dq_t[hr, r] = dq
    for n, grad in enumerate((dk_t, dv_t)):
        whole = grad[...].T
        kept[n] = whole[:half]
        sent[n] = whole[half:far].astype(BF16)
        to_prev[n] = whole[far : far + BLOCK].astype(BF16)
        to_next[n] = whole[far + BLOCK :].astype(BF16)


def remote(q, g, before, after, mine, theirs, partial, ends, width, depth, scale):
    rows, cols = q.shape
    pairs = cols // width
    hp = width // depth
    half = mine.shape[1]
    far = 2 * half
    wide = lambda n: pl.BlockSpec((n, width), lambda i, *_: (0, i))
    both = lambda n: pl.BlockSpec((2, n, width), lambda i, *_: (0, 0, i))
    fixed = pl.BlockSpec((3, hp, rows), lambda i, *_: (0, 0, 0))
    grid_spec = pltpu.PrefetchScalarGridSpec(
        num_scalar_prefetch=1,
        grid=(pairs,),
        in_specs=[wide(rows)] * 2 + [both(BLOCK)] * 2 + [both(half)] * 2 + [fixed] * pairs,
        out_specs=[
            both(half),
            both(half),
            both(BLOCK),
            both(BLOCK),
            pl.BlockSpec((width, rows), lambda i, *_: (i, 0)),
            pl.BlockSpec((None, 2, hp, rows), lambda i, *_: (i, 0, 0, 0)),
        ],
        scratch_shapes=[
            pltpu.VMEM((far, width), BF16),
            pltpu.VMEM((far, width), BF16),
            pltpu.VMEM((width, far), BF16),
            pltpu.VMEM((2, width, BLOCK), BF16),
            pltpu.VMEM((width, rows), BF16),
            pltpu.VMEM((width, rows), BF16),
            pltpu.VMEM((width, far + 2 * BLOCK), F32),
            pltpu.VMEM((width, far + 2 * BLOCK), F32),
        ],
    )
    return call(
        functools.partial(remote_body, depth, scale, pairs),
        "remote",
        flops=10 * (far * rows + 2 * BLOCK * BLOCK) * cols,
        moved=rows * cols * 8,
        grid_spec=grid_spec,
        out_shape=[
            struct((2, half, cols), F32),
            struct((2, half, cols), BF16),
            struct((2, BLOCK, cols), BF16),
            struct((2, BLOCK, cols), BF16),
            struct((cols, rows), F32),
            struct((pairs, 2, hp, rows), F32),
        ],
    )(ends, q, g, before, after, mine, theirs, *partial)


def local_body(depth, scale, chained, q, k, v, g, part, final, *rest):
    dq, dk, dv, k_t, q_t, g_t, dq_t, dk_t, dv_t = rest[3 if chained else 0 :]
    rows, width = q.shape
    blocks = rows // BLOCK
    k_t[...] = (k[...].astype(F32) * scale).astype(BF16).T
    q_t[...] = (q[...].astype(F32) * scale).astype(BF16).T
    g_t[...] = g[...].T
    for h, mask in enumerate(head_masks(width, depth)):
        hr = slice(h * depth, (h + 1) * depth)
        for b in range(blocks):
            r = slice(b * BLOCK, (b + 1) * BLOCK)
            qs = keep_head(q[r], mask, scale)
            gs = keep_head(g[r], mask)
            qt, gt = q_t[hr, r], g_t[hr, r]
            lse = final[0, h : h + 1, r]
            delta = final[1, h : h + 1, r]
            total = part[hr, r]
            for j in near(b, blocks):
                c = slice(j * BLOCK, (j + 1) * BLOCK)
                p = jnp.exp(dot(k[c], qs, NT) - lse)
                ds = (p * (dot(v[c], gs, NT) - delta)).astype(BF16)
                v_part = dot(gt, p.astype(BF16), NT)
                k_part = dot(qt, ds, NT)
                if b == near(j, blocks)[0]:
                    dv_t[hr, c] = v_part
                    dk_t[hr, c] = k_part
                else:
                    dv_t[hr, c] += v_part
                    dk_t[hr, c] += k_part
                total = total + dot(k_t[hr, c], ds, NN)
            dq_t[hr, r] = total
    dq[...] = dq_t[...].T.astype(BF16)
    dk[...] = dk_t[...].T
    dv[...] = dv_t[...].T


def local(q, k, v, g, part, final, before, width, depth, scale, pair):
    rows, cols = q.shape
    hp = width // depth
    column = pl.BlockSpec((rows, width), lambda i: (0, pair))
    chained = before is not None
    extra = list(before) if chained else []
    return call(
        functools.partial(local_body, depth, scale, chained),
        f"local{pair}",
        flops=10 * 3 * BLOCK * rows * width,
        moved=rows * width * 24,
        grid=(1,),
        in_specs=[column] * 4
        + [
            pl.BlockSpec((width, rows), lambda i: (pair, 0)),
            pl.BlockSpec((None, 2, hp, rows), lambda i: (pair, 0, 0, 0)),
        ]
        + [pl.BlockSpec(memory_space=pl.ANY)] * len(extra),
        out_specs=[column] * 3,
        out_shape=[struct((rows, cols), BF16), struct((rows, cols), F32), struct((rows, cols), F32)],
        scratch_shapes=[pltpu.VMEM((width, rows), BF16)] * 3 + [pltpu.VMEM((width, rows), F32)] * 3,
        input_output_aliases={6 + n: n for n in range(len(extra))},
    )(q, k, v, g, part, final, *extra)


def fold_body(rows1, rows2, only_whole, split_both, kept, got, next_kept, next_sent):
    for n in range(2):
        first = kept[n, :rows1]
        second = kept[n, rows1:]
        if only_whole:
            second = second + got[n].astype(F32)
        else:
            first = first + got[n, :rows1].astype(F32)
            second = second + got[n, rows1:].astype(F32)
        keep2 = rows2 // 2
        if split_both:
            keep1 = rows1 // 2
            next_kept[n] = jnp.concatenate([first[:keep1], second[:keep2]], axis=0)
            next_sent[n] = jnp.concatenate([first[keep1:], second[keep2:]], axis=0).astype(BF16)
        else:
            next_kept[n] = jnp.concatenate([first, second[:keep2]], axis=0)
            next_sent[n] = second[keep2:].astype(BF16)


def fold(kept, got, rows1, rows2, only_whole, split_both):
    cols = kept.shape[-1]
    if split_both:
        stay, go = (rows1 + rows2) // 2, (rows1 + rows2) // 2
    else:
        stay, go = rows1 + rows2 // 2, rows2 // 2
    return call(
        functools.partial(fold_body, rows1, rows2, only_whole, split_both),
        "fold",
        moved=kept.size * 8,
        out_shape=[struct((2, stay, cols), F32), struct((2, go, cols), BF16)],
    )(kept, got)


def finish_body(dk, dv, from_prev, from_next, kept, got, wide_group, wide_whole, out_k, out_v):
    block = pl.program_id(0)
    blocks = pl.num_programs(0)
    per = BLOCK // SEG1
    count1 = kept.shape[1] * SEG2 // (SEG1 + SEG2)
    low = jnp.where(block == 0, 1.0, 0.0)
    high = jnp.where(block == blocks - 1, 1.0, 0.0)
    for n, (src, dst) in enumerate(((dk, out_k), (dv, out_v))):
        sums = kept[n] + got[n].astype(F32)
        index = lax.broadcasted_iota(jnp.int32, (kept.shape[1], 1), 0)
        pieces = []
        whole = jnp.sum(jnp.where(index == count1 + block, sums, 0.0), axis=0, keepdims=True)
        for s in range(per):
            at = jnp.where(index == block * per + s, sums, 0.0)
            group = jnp.sum(at, axis=0, keepdims=True)
            c = slice(s * SEG1, (s + 1) * SEG1)
            piece = src[c] + group * wide_group[...] + whole * wide_whole[c]
            piece = piece + low * from_prev[n, c].astype(F32) + high * from_next[n, c].astype(F32)
            dst[c] = piece.astype(BF16)


def finish(dk, dv, from_prev, from_next, kept, got, wide_group, wide_whole):
    rows, cols = dk.shape
    tile = pl.BlockSpec((BLOCK, cols), lambda i: (i, 0))
    full = lambda x: pl.BlockSpec(x.shape, lambda i: (0,) * x.ndim)
    return call(
        finish_body,
        "finish",
        moved=rows * cols * 12,
        grid=(rows // BLOCK,),
        in_specs=[tile, tile]
        + [full(x) for x in (from_prev, from_next, kept, got, wide_group, wide_whole)],
        out_specs=[tile, tile],
        out_shape=[struct((rows, cols), BF16)] * 2,
    )(dk, dv, from_prev, from_next, kept, got, wide_group, wide_whole)


def shards(query, key, value, out_grad, pool_group, pool_global):
    rows, cols = query.shape
    heads = pool_group.shape[0]
    depth = cols // heads
    scale = 1.0 / math.sqrt(depth)
    width = 128 if cols % 128 == 0 and 128 % depth == 0 else cols
    pairs = cols // width
    devices = lax.axis_size("seq")
    position = lax.axis_index("seq")
    count1, count2 = rows // SEG1, rows // SEG2
    group_bits = list(range(1, GROUP.bit_length() - 1))
    other_bits = list(range(GROUP.bit_length() - 1, devices.bit_length() - 1))

    def swap(array, bit):
        return lax.ppermute(array, "seq", [(i, i ^ (1 << bit)) for i in range(devices)])

    def shift(array, by):
        pairs_ = [(i, i + by) for i in range(devices) if 0 <= i + by < devices]
        return lax.ppermute(array, "seq", pairs_)

    comb, first, last, wide_group, wide_whole = pool(key, value, pool_group, pool_global)
    ends = jnp.stack([position == 0, position == devices - 1]).astype(jnp.int32)

    before = after = None
    for bit in group_bits:
        got = swap(comb, bit)
        if before is None:
            before = shift(last, 1)
            after = shift(first, -1)
        comb = jnp.concatenate([comb, got], axis=0)
    whole = comb[:, :, count1 : count1 + count2]
    for bit in other_bits:
        whole = jnp.concatenate([whole, swap(whole, bit)], axis=0)
    slots1, slots2 = comb.shape[0], whole.shape[0]
    mine = pack(comb, whole, count1, count2)
    theirs = swap(mine, 0)

    partial = [stats(query, key, value, out_grad, width, depth, scale, p) for p in range(pairs)]
    kept, sent, to_prev, to_next, dq_t, final = remote(
        query, out_grad, before, after, mine, theirs, partial, ends, width, depth, scale
    )
    got = swap(sent, 0)
    from_next = shift(to_prev, -1)
    from_prev = shift(to_next, 1)

    rows1, rows2 = slots1 * count1, slots2 * count2
    only_whole = False
    for bit in reversed(other_bits):
        kept, sent = fold(kept, got, rows1, rows2, only_whole, False)
        rows2 //= 2
        got = swap(sent, bit)
        only_whole = True
    for bit in reversed(group_bits):
        kept, sent = fold(kept, got, rows1, rows2, only_whole, True)
        rows1 //= 2
        rows2 //= 2
        got = swap(sent, bit)
        only_whole = False

    grads = None
    for p in range(pairs):
        grads = local(
            query, key, value, out_grad, dq_t, final, grads, width, depth, scale, p
        )
    query_grad, dk, dv = grads
    key_grad, value_grad = finish(
        dk, dv, from_prev, from_next, kept, got, wide_group, wide_whole
    )
    return (query_grad, key_grad, value_grad)


def solution(mesh):
    rows = P("seq", "head")
    in_specs = (rows, rows, rows, rows, P("head", None), P("head", None))
    return jax.shard_map(
        shards, mesh=mesh, in_specs=in_specs, out_specs=(rows, rows, rows), check_vma=False
    )
```

```python
import functools
import math

import jax
import jax.numpy as jnp
from jax import lax
from jax.experimental import pallas as pl
from jax.experimental.pallas import tpu as pltpu
from jax.sharding import PartitionSpec as P

BLOCK = 256
SEG1 = 64
SEG2 = 256
GROUP = 8
NEG = -1e30
F32 = jnp.float32
BF16 = jnp.bfloat16
NT = (((1,), (1,)), ((), ()))
NN = (((1,), (0,)), ((), ()))
VMEM_LIMIT = 32 * 2**20
VMEM_ALL = 60 * 2**20
ANY = pl.BlockSpec(memory_space=pl.ANY)


def dot(a, b, dims):
    return lax.dot_general(a, b, dims, preferred_element_type=F32)


def struct(shape, dtype):
    return jax.ShapeDtypeStruct(shape, dtype)


def call(body, name, flops=0, moved=0, vmem=VMEM_LIMIT, **kwargs):
    cost = pl.CostEstimate(flops=int(flops), bytes_accessed=int(moved), transcendentals=0)
    params = pltpu.CompilerParams(vmem_limit_bytes=vmem)
    return pl.pallas_call(body, name=name, cost_estimate=cost, compiler_params=params, **kwargs)


def head_masks(width, depth):
    lane = lax.broadcasted_iota(jnp.int32, (1, width), 1)
    return [(lane >= h * depth) & (lane < (h + 1) * depth) for h in range(width // depth)]


def keep_head(rows, mask, scale=None):
    rows = jnp.where(mask, rows, 0)
    if scale is not None:
        rows = rows.astype(F32) * scale
    return rows.astype(BF16)


def near(block, blocks):
    return range(max(block - 1, 0), min(block + 2, blocks))


def edge_body(k, v, out):
    out[0] = k[...]
    out[1] = v[...]


def edge(k, v, block):
    cols = k.shape[1]
    spec = pl.BlockSpec((BLOCK, cols), lambda i: (block, 0))
    return call(
        edge_body,
        "edge",
        moved=8 * BLOCK * cols,
        vmem=VMEM_ALL,
        grid=(1,),
        in_specs=[spec, spec],
        out_specs=pl.BlockSpec((2, BLOCK, cols), lambda i: (0, 0, 0)),
        out_shape=struct((2, BLOCK, cols), BF16),
    )(k, v)


def pool_body(depth, k, v, group_pool, whole_pool, groups, wholes, first, wide_group, wide_whole):
    rows, width = k.shape
    heads = group_pool.shape[0]
    start = pl.program_id(0) * width
    head = lax.broadcasted_iota(jnp.int32, (heads, width), 0)
    col = lax.broadcasted_iota(jnp.int32, (heads, width), 1) + start
    pick = ((col >= head * depth) & (col < (head + 1) * depth)).astype(F32)
    for src, dst in ((group_pool, wide_group), (whole_pool, wide_whole)):
        dst[...] = lax.dot_general(
            src[...],
            pick,
            (((0,), (0,)), ((), ())),
            precision=lax.Precision.HIGHEST,
            preferred_element_type=F32,
        )
    for n, src in enumerate((k, v)):
        first[n] = src[:BLOCK]
        for segment, wide, dst in ((SEG1, wide_group, groups), (SEG2, wide_whole, wholes)):
            sums = []
            for s in range(rows // segment):
                part = src[s * segment : (s + 1) * segment].astype(F32) * wide[...]
                sums.append(jnp.sum(part, axis=0, keepdims=True))
            dst[n] = jnp.concatenate(sums, axis=0).astype(BF16)


def pool(k, v, group_pool, whole_pool, width):
    rows, cols = k.shape
    heads = group_pool.shape[0]
    count1, count2 = rows // SEG1, rows // SEG2
    column = lambda n: pl.BlockSpec((n, width), lambda i: (0, i))
    both = lambda n: pl.BlockSpec((2, n, width), lambda i: (0, 0, i))
    full = lambda x: pl.BlockSpec(x.shape, lambda i: (0, 0))
    return call(
        functools.partial(pool_body, cols // heads),
        "pool",
        moved=k.size * 6,
        vmem=VMEM_ALL,
        grid=(cols // width,),
        in_specs=[column(rows), column(rows), full(group_pool), full(whole_pool)],
        out_specs=[both(count1), both(count2), both(BLOCK), column(SEG1), column(SEG2)],
        out_shape=[
            struct((2, count1, cols), BF16),
            struct((2, count2, cols), BF16),
            struct((2, BLOCK, cols), BF16),
            struct((SEG1, cols), F32),
            struct((SEG2, cols), F32),
        ],
    )(k, v, group_pool, whole_pool)


def join_body(axis, has_token, *refs):
    parts, out = refs[: len(refs) - 1 - has_token], refs[-1]
    at = 0
    for part in parts:
        size = part.shape[axis]
        if axis == 0:
            out[at : at + size] = part[...]
            at += size
    if axis == 1:
        for n in range(2):
            rows = [part[n].astype(F32) for part in parts]
            out[n] = jnp.concatenate(rows, axis=0).astype(BF16)


def join(parts, axis, token=None):
    shape = list(parts[0].shape)
    shape[axis] = sum(part.shape[axis] for part in parts)
    tokens = [] if token is None else [token]
    return call(
        functools.partial(join_body, axis, len(tokens)),
        "join",
        moved=4 * math.prod(shape),
        in_specs=[pl.BlockSpec(memory_space=pltpu.VMEM)] * len(parts) + [ANY] * len(tokens),
        out_shape=struct(tuple(shape), BF16),
    )(*parts, *tokens)


def stats_body(depth, scale, q, k, v, g, out):
    rows, width = q.shape
    blocks = rows // BLOCK
    chunk = 64
    for h, mask in enumerate(head_masks(width, depth)):
        for b in range(blocks):
            r = slice(b * BLOCK, (b + 1) * BLOCK)
            qs = keep_head(q[r], mask, scale)
            gs = keep_head(g[r], mask)
            lo, hi = near(b, blocks)[0] * BLOCK, (near(b, blocks)[-1] + 1) * BLOCK
            s_all = dot(k[lo:hi], qs, NT)
            d_all = dot(v[lo:hi], gs, NT)
            top = total = inner = None
            for c in range(0, hi - lo, chunk):
                s = s_all[c : c + chunk].reshape(chunk // 8, 8, BLOCK)
                d = d_all[c : c + chunk].reshape(chunk // 8, 8, BLOCK)
                here = jnp.max(s, axis=0)
                if top is None:
                    new = here
                else:
                    new = jnp.maximum(top, here)
                e = jnp.exp(s - new[None])
                sum_e = jnp.sum(e, axis=0)
                sum_d = jnp.sum(e * d, axis=0)
                if top is not None:
                    fade = jnp.exp(top - new)
                    sum_e = sum_e + total * fade
                    sum_d = sum_d + inner * fade
                top, total, inner = new, sum_e, sum_d
            most = jnp.max(top, axis=0, keepdims=True)
            fade = jnp.exp(top - most)
            out[0, h : h + 1, r] = most
            out[1, h : h + 1, r] = jnp.sum(total * fade, axis=0, keepdims=True)
            out[2, h : h + 1, r] = jnp.sum(inner * fade, axis=0, keepdims=True)


def stats(q, k, v, g, width, depth, scale, pair):
    rows = q.shape[0]
    hp = width // depth
    cols = pl.BlockSpec((rows, width), lambda i: (0, pair))
    return call(
        functools.partial(stats_body, depth, scale),
        f"stats{pair}",
        flops=2 * 2 * 3 * BLOCK * rows * width,
        moved=rows * width * 8,
        grid=(1,),
        in_specs=[cols] * 4,
        out_specs=pl.BlockSpec((3, hp, rows), lambda i: (0, 0, 0)),
        out_shape=struct((3, hp, rows), F32),
    )(q, k, v, g)


def remote_body(depth, scale, pairs, ends, q, g, before, after, mine, theirs, *rest):
    partial = rest[:pairs]
    kept, sent, to_prev, to_next, dq_t, final, far_k, far_v = rest[pairs : pairs + 8]
    far_kt, near_t, far_dk, far_dv, near_d = rest[pairs + 8 :]
    rows, width = q.shape
    blocks = rows // BLOCK
    slots, _, per, _ = mine.shape
    half = slots * per
    pair = pl.program_id(0)
    for n, far in enumerate((far_k, far_v)):
        pieces = [src[s, n].astype(F32) for src in (mine, theirs) for s in range(slots)]
        far[...] = jnp.concatenate(pieces, axis=0).astype(BF16)
    far_kt[...] = (far_k[...].astype(F32) * scale).astype(BF16).T
    near_t[0] = (before[0].astype(F32) * scale).astype(BF16).T
    near_t[1] = (after[0].astype(F32) * scale).astype(BF16).T
    low = jnp.where(ends[0] == 1, NEG, 0.0)
    high = jnp.where(ends[1] == 1, NEG, 0.0)
    for h, mask in enumerate(head_masks(width, depth)):
        hr = slice(h * depth, (h + 1) * depth)
        for b in range(blocks):
            r = slice(b * BLOCK, (b + 1) * BLOCK)
            qs = keep_head(q[r], mask, scale)
            gs = keep_head(g[r], mask)
            scores = [dot(far_k[...], qs, NT)]
            values = [dot(far_v[...], gs, NT)]
            turned = [far_kt[hr]]
            sinks = [(far_dk, far_dv)]
            if b == 0:
                scores.append(dot(before[0], qs, NT) + low)
                values.append(dot(before[1], gs, NT))
                turned.append(near_t[0, hr])
                sinks.append((near_d.at[0], near_d.at[1]))
            if b == blocks - 1:
                scores.append(dot(after[0], qs, NT) + high)
                values.append(dot(after[1], gs, NT))
                turned.append(near_t[1, hr])
                sinks.append((near_d.at[2], near_d.at[3]))
            old = [partial[0][n, h : h + 1, r] for n in range(3)]
            for n in range(1, pairs):
                old = [
                    jnp.where(pair == n, partial[n][m, h : h + 1, r], old[m]) for m in range(3)
                ]
            top = old[0]
            for s in scores:
                top = jnp.maximum(top, jnp.max(s, axis=0, keepdims=True))
            fade = jnp.exp(old[0] - top)
            total = old[1] * fade
            inner = old[2] * fade
            exps = []
            for s, d in zip(scores, values):
                e = jnp.exp(s - top)
                exps.append(e)
                total = total + jnp.sum(e, axis=0, keepdims=True)
                inner = inner + jnp.sum(e * d, axis=0, keepdims=True)
            share = 1.0 / total
            delta = inner * share
            final[0, h : h + 1, r] = top + jnp.log(total)
            final[1, h : h + 1, r] = delta
            dq = None
            for n, (e, d, kt, (dk, dv)) in enumerate(zip(exps, values, turned, sinks)):
                p = e * share
                ds = (p * (d - delta)).astype(BF16)
                v_part = dot(p.astype(BF16), gs, NN)
                k_part = dot(ds, qs, NN)
                if h == 0 and (n or b == 0):
                    dv[...] = v_part
                    dk[...] = k_part
                else:
                    dv[...] += v_part
                    dk[...] += k_part
                part = dot(kt, ds, NN)
                dq = part if dq is None else dq + part
            dq_t[hr, r] = dq
    for n, far in enumerate((far_dk, far_dv)):
        kept[n] = far[:half]
        sent[n] = far[half:].astype(BF16)
        to_prev[n] = near_d[n].astype(BF16)
        to_next[n] = near_d[2 + n].astype(BF16)


def remote(q, g, before, after, mine, theirs, partial, ends, width, depth, scale):
    rows, cols = q.shape
    pairs = cols // width
    hp = width // depth
    slots, _, per, _ = mine.shape
    half = slots * per
    far = 2 * half
    wide = lambda n: pl.BlockSpec((n, width), lambda i, *_: (0, i))
    both = lambda n: pl.BlockSpec((2, n, width), lambda i, *_: (0, 0, i))
    slot = pl.BlockSpec((slots, 2, per, width), lambda i, *_: (0, 0, 0, i))
    fixed = pl.BlockSpec((3, hp, rows), lambda i, *_: (0, 0, 0))
    grid_spec = pltpu.PrefetchScalarGridSpec(
        num_scalar_prefetch=1,
        grid=(pairs,),
        in_specs=[wide(rows)] * 2 + [both(BLOCK)] * 2 + [slot] * 2 + [fixed] * pairs,
        out_specs=[
            both(half),
            both(half),
            both(BLOCK),
            both(BLOCK),
            pl.BlockSpec((width, rows), lambda i, *_: (i, 0)),
            pl.BlockSpec((None, 2, hp, rows), lambda i, *_: (i, 0, 0, 0)),
        ],
        scratch_shapes=[
            pltpu.VMEM((far, width), BF16),
            pltpu.VMEM((far, width), BF16),
            pltpu.VMEM((width, far), BF16),
            pltpu.VMEM((2, width, BLOCK), BF16),
            pltpu.VMEM((far, width), F32),
            pltpu.VMEM((far, width), F32),
            pltpu.VMEM((4, BLOCK, width), F32),
        ],
    )
    return call(
        functools.partial(remote_body, depth, scale, pairs),
        "remote",
        flops=10 * (far * rows + 2 * BLOCK * BLOCK) * cols,
        moved=rows * cols * 8,
        grid_spec=grid_spec,
        out_shape=[
            struct((2, half, cols), F32),
            struct((2, half, cols), BF16),
            struct((2, BLOCK, cols), BF16),
            struct((2, BLOCK, cols), BF16),
            struct((cols, rows), F32),
            struct((pairs, 2, hp, rows), F32),
        ],
    )(ends, q, g, before, after, mine, theirs, *partial)


def local_body(depth, scale, chained, q, k, v, g, part, final, *rest):
    dq, dk, dv, k_t, dq_t = rest[chained:]
    rows, width = q.shape
    blocks = rows // BLOCK
    k_t[...] = (k[...].astype(F32) * scale).astype(BF16).T
    for h, mask in enumerate(head_masks(width, depth)):
        hr = slice(h * depth, (h + 1) * depth)
        for b in range(blocks):
            r = slice(b * BLOCK, (b + 1) * BLOCK)
            qs = keep_head(q[r], mask, scale)
            gs = keep_head(g[r], mask)
            reach = near(b, blocks)
            c = slice(reach[0] * BLOCK, (reach[-1] + 1) * BLOCK)
            p = jnp.exp(dot(k[c], qs, NT) - final[0, h : h + 1, r])
            ds = (p * (dot(v[c], gs, NT) - final[1, h : h + 1, r])).astype(BF16)
            v_part = dot(p.astype(BF16), gs, NN)
            k_part = dot(ds, qs, NN)
            for n, j in enumerate(reach):
                rj = slice(j * BLOCK, (j + 1) * BLOCK)
                here = slice(n * BLOCK, (n + 1) * BLOCK)
                if h == 0 and b == near(j, blocks)[0]:
                    dv[rj] = v_part[here]
                    dk[rj] = k_part[here]
                else:
                    dv[rj] += v_part[here]
                    dk[rj] += k_part[here]
            dq_t[hr, r] = part[hr, r] + dot(k_t[hr, c], ds, NN)
    dq[...] = dq_t[...].T.astype(BF16)


def local(q, k, v, g, part, final, before, width, depth, scale, pair):
    rows, cols = q.shape
    hp = width // depth
    column = pl.BlockSpec((rows, width), lambda i: (0, pair))
    alone = pl.BlockSpec((rows, width), lambda i: (0, 0))
    extra = [] if before is None else [before]
    return call(
        functools.partial(local_body, depth, scale, len(extra)),
        f"local{pair}",
        flops=10 * 3 * BLOCK * rows * width,
        moved=rows * width * 24,
        grid=(1,),
        in_specs=[column] * 4
        + [
            pl.BlockSpec((width, rows), lambda i: (pair, 0)),
            pl.BlockSpec((None, 2, hp, rows), lambda i: (pair, 0, 0, 0)),
        ]
        + [ANY] * len(extra),
        out_specs=[column, alone, alone],
        out_shape=[struct((rows, cols), BF16)] + [struct((rows, width), F32)] * 2,
        scratch_shapes=[pltpu.VMEM((width, rows), BF16), pltpu.VMEM((width, rows), F32)],
        input_output_aliases={6: 0} if extra else {},
    )(q, k, v, g, part, final, *extra)


def fold_body(at, cut, kept, got, *rest):
    next_kept, next_sent = rest[-2:]
    for n in range(2):
        rows = kept[n, at:] + got[n].astype(F32)
        if at:
            rows = jnp.concatenate([kept[n, :at], rows], axis=0)
        next_kept[n] = rows[:cut]
        next_sent[n] = rows[cut:].astype(BF16)


def fold(kept, got, cut, tokens=(), passed=()):
    cols = kept.shape[-1]
    rows = kept.shape[1]
    at = rows - got.shape[1]
    vmem = pl.BlockSpec(memory_space=pltpu.VMEM)
    extra = list(passed) + list(tokens)

    def body(kept, got, *rest):
        fold_body(at, cut, kept, got, *rest[len(extra) : len(extra) + 2])

    return call(
        body,
        "fold",
        moved=kept.size * 8,
        in_specs=[vmem, vmem] + [ANY] * len(extra),
        out_specs=[vmem, vmem] + [ANY] * len(passed),
        out_shape=[struct((2, cut, cols), F32), struct((2, rows - cut, cols), BF16)]
        + [struct(x.shape, x.dtype) for x in passed],
        input_output_aliases={2 + n: 2 + n for n in range(len(passed))},
    )(kept, got, *extra)


def finish_body(pairs, *refs):
    dk, dv = refs[:pairs], refs[pairs : 2 * pairs]
    from_prev, from_next, kept, got, wide_group, wide_whole, out_k, out_v = refs[2 * pairs :]
    block = pl.program_id(0)
    blocks = pl.num_programs(0)
    width = dk[0].shape[1]
    per = BLOCK // SEG1
    rows = kept.shape[1]
    at = rows - got.shape[1]
    count1 = rows * SEG2 // (SEG1 + SEG2)
    low = jnp.where(block == 0, 1.0, 0.0)
    high = jnp.where(block == blocks - 1, 1.0, 0.0)
    index = lax.broadcasted_iota(jnp.int32, (rows, 1), 0)
    for n, (src, dst) in enumerate(((dk, out_k), (dv, out_v))):
        sums = kept[n, at:] + got[n].astype(F32)
        if at:
            sums = jnp.concatenate([kept[n, :at], sums], axis=0)
        whole = jnp.sum(jnp.where(index == count1 + block, sums, 0.0), axis=0, keepdims=True)
        for s in range(per):
            mine = jnp.where(index == block * per + s, sums, 0.0)
            group = jnp.sum(mine, axis=0, keepdims=True)
            c = slice(s * SEG1, (s + 1) * SEG1)
            piece = group * wide_group[...] + whole * wide_whole[c]
            piece = piece + low * from_prev[n, c].astype(F32) + high * from_next[n, c].astype(F32)
            for p in range(pairs):
                lanes = slice(p * width, (p + 1) * width)
                dst[c, lanes] = (piece[:, lanes] + src[p][c]).astype(BF16)


def finish(dk, dv, from_prev, from_next, kept, got, wide_group, wide_whole):
    rows, width = dk[0].shape
    pairs = len(dk)
    cols = width * pairs
    tile = pl.BlockSpec((BLOCK, cols), lambda i: (i, 0))
    narrow = pl.BlockSpec((BLOCK, width), lambda i: (i, 0))
    full = lambda x: pl.BlockSpec(x.shape, lambda i: (0,) * x.ndim)
    return call(
        functools.partial(finish_body, pairs),
        "finish",
        moved=rows * cols * 12,
        grid=(rows // BLOCK,),
        in_specs=[narrow] * (2 * pairs)
        + [full(x) for x in (from_prev, from_next, kept, got, wide_group, wide_whole)],
        out_specs=[tile, tile],
        out_shape=[struct((rows, cols), BF16)] * 2,
    )(*dk, *dv, from_prev, from_next, kept, got, wide_group, wide_whole)


def shards(query, key, value, out_grad, pool_group, pool_global):
    rows, cols = query.shape
    heads = pool_group.shape[0]
    depth = cols // heads
    scale = 1.0 / math.sqrt(depth)
    width = 128 if cols % 128 == 0 and 128 % depth == 0 else cols
    pairs = cols // width
    devices = lax.axis_size("seq")
    position = lax.axis_index("seq")
    count1, count2 = rows // SEG1, rows // SEG2
    group_bits = list(range(1, GROUP.bit_length() - 1))
    other_bits = list(range(GROUP.bit_length() - 1, devices.bit_length() - 1))

    def swap(array, bit):
        return lax.ppermute(array, "seq", [(i, i ^ (1 << bit)) for i in range(devices)])

    def shift(array, by):
        route = [(i, i + by) for i in range(devices) if 0 <= i + by < devices]
        return lax.ppermute(array, "seq", route)

    before = shift(edge(key, value, rows // BLOCK - 1), 1)
    groups, wholes, first, wide_group, wide_whole = pool(
        key, value, pool_group, pool_global, width
    )
    ends = jnp.stack([position == 0, position == devices - 1]).astype(jnp.int32)
    partial = [
        stats(query, key, value, out_grad, width, depth, scale, p) for p in range(pairs)
    ]
    waiting = list(partial)

    def token():
        return waiting.pop(0) if waiting else None

    for n, bit in enumerate(other_bits):
        got = swap(wholes, bit)
        if n < len(other_bits) - 1:
            wholes = join([wholes, got], 1)
    parts = [groups, wholes] + ([got] if other_bits else [])
    comb = join(parts, 1, token())[None]
    after = None
    for bit in group_bits:
        got = swap(comb, bit)
        if after is None:
            after = shift(first, -1)
        comb = join([comb, got], 0, token())
    theirs = swap(comb, 0)

    kept, sent, to_prev, to_next, dq_t, final = remote(
        query, out_grad, before, after, comb, theirs, partial, ends, width, depth, scale
    )
    got = swap(sent, 0)
    from_next = shift(to_prev, -1)

    query_grad, dk, dv = None, [], []

    def step():
        nonlocal query_grad
        if len(dk) == pairs:
            return []
        query_grad, a, b = local(
            query, key, value, out_grad, dq_t, final, query_grad, width, depth, scale, len(dk)
        )
        dk.append(a)
        dv.append(b)
        return [a]

    from_prev = None
    for bit in list(reversed(group_bits)) + list(reversed(other_bits)):
        size = kept.shape[1]
        if bit in group_bits:
            cut = size // 2
        else:
            cut = count1 + (size - count1) // 2
        if from_prev is None:
            kept, sent, to_next = fold(kept, got, cut, step(), [to_next])
            got = swap(sent, bit)
            from_prev = shift(to_next, 1)
        else:
            kept, sent = fold(kept, got, cut, step())
            got = swap(sent, bit)
    while len(dk) < pairs:
        step()
    key_grad, value_grad = finish(
        dk, dv, from_prev, from_next, kept, got, wide_group, wide_whole
    )
    return (query_grad, key_grad, value_grad)


def solution(mesh):
    rows = P("seq", "head")
    in_specs = (rows, rows, rows, rows, P("head", None), P("head", None))
    return jax.shard_map(
        shards, mesh=mesh, in_specs=in_specs, out_specs=(rows, rows, rows), check_vma=False
    )
```

```python
import functools
import math

import jax
import jax.numpy as jnp
from jax import lax
from jax.experimental import pallas as pl
from jax.experimental.pallas import tpu as pltpu
from jax.sharding import PartitionSpec as P


BLOCK = 256
SEG1 = 64
SEG2 = 256
GROUP = 8
NEG = -1e30
F32 = jnp.float32
BF16 = jnp.bfloat16
NT = (((1,), (1,)), ((), ()))
NN = (((1,), (0,)), ((), ()))
VMEM_LIMIT = 32 * 2**20
VMEM_ALL = 60 * 2**20
ANY = pl.BlockSpec(memory_space=pl.ANY)


def dot(a, b, dims):
    return lax.dot_general(a, b, dims, preferred_element_type=F32)


def struct(shape, dtype):
    return jax.ShapeDtypeStruct(shape, dtype)


def call(body, flops=0, moved=0, vmem=VMEM_LIMIT, **kwargs):
    cost = pl.CostEstimate(flops=int(flops), bytes_accessed=int(moved), transcendentals=0)
    params = pltpu.CompilerParams(vmem_limit_bytes=vmem)
    return pl.pallas_call(body, cost_estimate=cost, compiler_params=params, **kwargs)


def head_masks(width, depth):
    lane = lax.broadcasted_iota(jnp.int32, (1, width), 1)
    return [(lane >= h * depth) & (lane < (h + 1) * depth) for h in range(width // depth)]


def keep_head(rows, mask, scale=None):
    rows = jnp.where(mask, rows, 0)
    if scale is not None:
        rows = rows.astype(F32) * scale
    return rows.astype(BF16)


def near(block, blocks):
    return range(max(block - 1, 0), min(block + 2, blocks))


def pool_body(
    depth, ends, k, v, group_pool, whole_pool, groups, wholes, inner, outer, wide_group, wide_whole
):
    rows, width = k.shape
    heads = group_pool.shape[0]
    start = pl.program_id(0) * width
    head = lax.broadcasted_iota(jnp.int32, (heads, width), 0)
    col = lax.broadcasted_iota(jnp.int32, (heads, width), 1) + start
    pick = ((col >= head * depth) & (col < (head + 1) * depth)).astype(F32)
    for src, dst in ((group_pool, wide_group), (whole_pool, wide_whole)):
        dst[...] = lax.dot_general(
            src[...],
            pick,
            (((0,), (0,)), ((), ())),
            precision=lax.Precision.HIGHEST,
            preferred_element_type=F32,
        )
    odd = ends[2]
    low = pl.multiple_of(odd * (rows - BLOCK), BLOCK)
    high = pl.multiple_of((1 - odd) * (rows - BLOCK), BLOCK)
    for n, src in enumerate((k, v)):
        inner[n] = src[pl.ds(high, BLOCK)]
        outer[n] = src[pl.ds(low, BLOCK)]
        for segment, wide, dst in ((SEG1, wide_group, groups), (SEG2, wide_whole, wholes)):
            sums = []
            for s in range(rows // segment):
                part = src[s * segment : (s + 1) * segment].astype(F32) * wide[...]
                sums.append(jnp.sum(part, axis=0, keepdims=True))
            dst[n] = jnp.concatenate(sums, axis=0).astype(BF16)


def pool(k, v, group_pool, whole_pool, ends, width):
    rows, cols = k.shape
    heads = group_pool.shape[0]
    count1, count2 = rows // SEG1, rows // SEG2
    column = lambda n: pl.BlockSpec((n, width), lambda i, *_: (0, i))
    both = lambda n: pl.BlockSpec((2, n, width), lambda i, *_: (0, 0, i))
    full = lambda x: pl.BlockSpec(x.shape, lambda i, *_: (0, 0))
    return call(
        functools.partial(pool_body, cols // heads),
        moved=k.size * 6,
        vmem=VMEM_ALL,
        grid_spec=pltpu.PrefetchScalarGridSpec(
            num_scalar_prefetch=1,
            grid=(cols // width,),
            in_specs=[column(rows), column(rows), full(group_pool), full(whole_pool)],
            out_specs=[both(count1), both(count2), both(BLOCK), both(BLOCK)]
            + [column(SEG1), column(SEG2)],
        ),
        out_shape=[
            struct((2, count1, cols), BF16),
            struct((2, count2, cols), BF16),
            struct((2, BLOCK, cols), BF16),
            struct((2, BLOCK, cols), BF16),
            struct((SEG1, cols), F32),
            struct((SEG2, cols), F32),
        ],
    )(ends, k, v, group_pool, whole_pool)


def join(slots, tokens=(), passed=()):
    flat, plan, count, rows = [], [], 0, 0
    for slot in slots:
        if isinstance(slot, list):
            plan.append((count, len(slot)))
            flat += slot
            rows = sum(part.shape[1] for part in slot)
            count += 1
        else:
            plan.append((count, 0))
            flat.append(slot)
            rows = slot.shape[2]
            count += slot.shape[0]
    cols = flat[0].shape[-1]
    extra = list(passed) + list(tokens)

    def body(*refs):
        out = refs[len(flat) + len(extra)]
        at = 0
        for start, parts in plan:
            if not parts:
                out[start : start + refs[at].shape[0]] = refs[at][...]
                at += 1
                continue
            for n in range(2):
                pieces = [refs[at + i][n].astype(F32) for i in range(parts)]
                out[start, n] = jnp.concatenate(pieces, axis=0).astype(BF16)
            at += parts

    vmem = pl.BlockSpec(memory_space=pltpu.VMEM)
    return call(
        body,
        moved=4 * count * 2 * rows * cols,
        in_specs=[vmem] * len(flat) + [ANY] * len(extra),
        out_specs=[vmem] + [ANY] * len(passed),
        out_shape=[struct((count, 2, rows, cols), BF16)]
        + [struct(x.shape, x.dtype) for x in passed],
        input_output_aliases={len(flat) + n: 1 + n for n in range(len(passed))},
    )(*flat, *extra)


def merge(state, s_all, d_all, chunk=64):
    for c in range(0, s_all.shape[0], chunk):
        s = s_all[c : c + chunk]
        count = s.shape[0] // 8
        s = s.reshape(count, 8, s.shape[1])
        d = d_all[c : c + chunk].reshape(s.shape)
        here = jnp.max(s, axis=0)
        top = here if state is None else jnp.maximum(state[0], here)
        e = jnp.exp(s - top[None])
        total = jnp.sum(e, axis=0)
        inner = jnp.sum(e * d, axis=0)
        if state is not None:
            fade = jnp.exp(state[0] - top)
            total = total + state[1] * fade
            inner = inner + state[2] * fade
        state = (top, total, inner)
    return state


def stats_body(depth, scale, q, k, v, g, out):
    rows, width = q.shape
    blocks = rows // BLOCK
    for h, mask in enumerate(head_masks(width, depth)):
        for b in range(blocks):
            r = slice(b * BLOCK, (b + 1) * BLOCK)
            qs = keep_head(q[r], mask, scale)
            gs = keep_head(g[r], mask)
            c = slice(near(b, blocks)[0] * BLOCK, (near(b, blocks)[-1] + 1) * BLOCK)
            top, total, inner = merge(None, dot(k[c], qs, NT), dot(v[c], gs, NT))
            most = jnp.max(top, axis=0, keepdims=True)
            fade = jnp.exp(top - most)
            out[0, h : h + 1, r] = most
            out[1, h : h + 1, r] = jnp.sum(total * fade, axis=0, keepdims=True)
            out[2, h : h + 1, r] = jnp.sum(inner * fade, axis=0, keepdims=True)


def stats(q, k, v, g, width, depth, scale, pair):
    rows = q.shape[0]
    hp = width // depth
    cols = pl.BlockSpec((rows, width), lambda i: (0, pair))
    return call(
        functools.partial(stats_body, depth, scale),
        flops=2 * 2 * 3 * BLOCK * rows * width,
        moved=rows * width * 8,
        grid=(1,),
        in_specs=[cols] * 4,
        out_specs=pl.BlockSpec((3, hp, rows), lambda i: (0, 0, 0)),
        out_shape=struct((3, hp, rows), F32),
    )(q, k, v, g)


def remote_body(depth, scale, pairs, ends, q, g, inner, outer, mine, theirs, *rest):
    partial = rest[:pairs]
    kept, sent, inner_d, outer_d, dq_t, final = rest[pairs : pairs + 6]
    far_k, far_v, far_kt, near_t, far_dk, far_dv, near_d, qs, gs, s_all, d_all = rest[pairs + 6 :]
    rows, width = q.shape
    blocks = rows // BLOCK
    slots, _, per, _ = mine.shape
    half = slots * per
    pair = pl.program_id(0)
    masks = head_masks(width, depth)
    for n, far in enumerate((far_k, far_v)):
        for m, src in enumerate((mine, theirs)):
            for s in range(slots):
                at = m * half + s * per
                far[at : at + per] = src[s, n]
    far_kt[...] = (far_k[...].astype(F32) * scale).astype(BF16).T
    near_t[0] = (inner[0].astype(F32) * scale).astype(BF16).T
    near_t[1] = (outer[0].astype(F32) * scale).astype(BF16).T
    scaled = (q[...].astype(F32) * scale).astype(BF16)
    for h, mask in enumerate(masks):
        qs[h] = jnp.where(mask, scaled, 0).astype(BF16)
        gs[h] = jnp.where(mask, g[...], 0).astype(BF16)
    odd = ends[2]
    missing = jnp.where((ends[0] == 1) | (ends[1] == 1), NEG, 0.0)
    first = (1 - odd) * (blocks - 1)
    last = odd * (blocks - 1)
    middle = list(range(1, blocks - 1))
    order = [first, last] + middle if blocks > 1 else [0]

    def place(n):
        return pl.ds(pl.multiple_of(order[n] * BLOCK, BLOCK), BLOCK)

    def sets(n):
        out = [(0, far_k, far_v, None, far_kt, far_dk, far_dv)]
        if n == 0:
            out.append(
                (2 * half, inner.at[0], inner.at[1], None, near_t.at[0], near_d.at[0], near_d.at[1])
            )
        if n == (1 if blocks > 1 else 0):
            out.append(
                (
                    2 * half + BLOCK,
                    outer.at[0],
                    outer.at[1],
                    missing,
                    near_t.at[1],
                    near_d.at[2],
                    near_d.at[3],
                )
            )
        return out

    for h in range(len(masks)):
        for b in range(blocks):
            r = place(b)
            old = [partial[0][m, h : h + 1, r] for m in range(3)]
            for n in range(1, pairs):
                old = [
                    jnp.where(pair == n, partial[n][m, h : h + 1, r], old[m]) for m in range(3)
                ]
            state = None
            for at, keys, vals, bias, *_ in sets(b):
                size = keys.shape[0]
                s = dot(keys[...], qs[h, r], NT)
                d = dot(vals[...], gs[h, r], NT)
                if bias is not None:
                    s = s + bias
                s_all[h * blocks + b, at : at + size] = s
                d_all[h * blocks + b, at : at + size] = d
                state = merge(state, s, d)
            top8, total8, inner8 = state
            top = jnp.maximum(old[0], jnp.max(top8, axis=0, keepdims=True))
            fade = jnp.exp(old[0] - top)
            fade8 = jnp.exp(top8 - top)
            total = old[1] * fade + jnp.sum(total8 * fade8, axis=0, keepdims=True)
            dots = old[2] * fade + jnp.sum(inner8 * fade8, axis=0, keepdims=True)
            final[0, h : h + 1, r] = top + jnp.log(total)
            final[1, h : h + 1, r] = dots / total
    for h in range(len(masks)):
        hr = slice(h * depth, (h + 1) * depth)
        for b in range(blocks):
            r = place(b)
            lse = final[0, h : h + 1, r]
            delta = final[1, h : h + 1, r]
            dq = None
            for n, (at, keys, _, _, turned, dk, dv) in enumerate(sets(b)):
                size = keys.shape[0]
                p = jnp.exp(s_all[h * blocks + b, at : at + size] - lse)
                ds = (p * (d_all[h * blocks + b, at : at + size] - delta)).astype(BF16)
                v_part = dot(p.astype(BF16), gs[h, r], NN)
                k_part = dot(ds, qs[h, r], NN)
                if h == 0 and (n or b == 0):
                    dv[...] = v_part
                    dk[...] = k_part
                else:
                    dv[...] += v_part
                    dk[...] += k_part
                part = dot(turned[hr], ds, NN)
                dq = part if dq is None else dq + part
            dq_t[hr, r] = dq
    for n, far in enumerate((far_dk, far_dv)):
        kept[n] = far[:half]
        sent[n] = far[half:].astype(BF16)
        inner_d[n] = near_d[n].astype(BF16)
        outer_d[n] = near_d[2 + n].astype(BF16)


def remote(q, g, inner, outer, mine, theirs, partial, ends, width, depth, scale):
    rows, cols = q.shape
    pairs = cols // width
    hp = width // depth
    slots, _, per, _ = mine.shape
    half = slots * per
    far = 2 * half
    wide = lambda n: pl.BlockSpec((n, width), lambda i, *_: (0, i))
    both = lambda n: pl.BlockSpec((2, n, width), lambda i, *_: (0, 0, i))
    slot = pl.BlockSpec((slots, 2, per, width), lambda i, *_: (0, 0, 0, i))
    fixed = pl.BlockSpec((3, hp, rows), lambda i, *_: (0, 0, 0))
    held = pltpu.VMEM((hp * rows // BLOCK, far + 2 * BLOCK, BLOCK), F32)
    grid_spec = pltpu.PrefetchScalarGridSpec(
        num_scalar_prefetch=1,
        grid=(pairs,),
        in_specs=[wide(rows)] * 2 + [both(BLOCK)] * 2 + [slot] * 2 + [fixed] * pairs,
        out_specs=[
            both(half),
            both(half),
            both(BLOCK),
            both(BLOCK),
            pl.BlockSpec((width, rows), lambda i, *_: (i, 0)),
            pl.BlockSpec((None, 2, hp, rows), lambda i, *_: (i, 0, 0, 0)),
        ],
        scratch_shapes=[
            pltpu.VMEM((far, width), BF16),
            pltpu.VMEM((far, width), BF16),
            pltpu.VMEM((width, far), BF16),
            pltpu.VMEM((2, width, BLOCK), BF16),
            pltpu.VMEM((far, width), F32),
            pltpu.VMEM((far, width), F32),
            pltpu.VMEM((4, BLOCK, width), F32),
            pltpu.VMEM((hp, rows, width), BF16),
            pltpu.VMEM((hp, rows, width), BF16),
            held,
            held,
        ],
    )
    return call(
        functools.partial(remote_body, depth, scale, pairs),
        flops=10 * (far * rows + 2 * BLOCK * BLOCK) * cols,
        moved=rows * cols * 8,
        grid_spec=grid_spec,
        out_shape=[
            struct((2, half, cols), F32),
            struct((2, half, cols), BF16),
            struct((2, BLOCK, cols), BF16),
            struct((2, BLOCK, cols), BF16),
            struct((cols, rows), F32),
            struct((pairs, 2, hp, rows), F32),
        ],
    )(ends, q, g, inner, outer, mine, theirs, *partial)


def local_body(depth, scale, chained, q, k, v, g, part, final, *rest):
    dq, dk, dv, k_t, dq_t = rest[chained:]
    rows, width = q.shape
    blocks = rows // BLOCK
    k_t[...] = (k[...].astype(F32) * scale).astype(BF16).T
    for h, mask in enumerate(head_masks(width, depth)):
        hr = slice(h * depth, (h + 1) * depth)
        for b in range(blocks):
            r = slice(b * BLOCK, (b + 1) * BLOCK)
            qs = keep_head(q[r], mask, scale)
            gs = keep_head(g[r], mask)
            reach = near(b, blocks)
            c = slice(reach[0] * BLOCK, (reach[-1] + 1) * BLOCK)
            p = jnp.exp(dot(k[c], qs, NT) - final[0, h : h + 1, r])
            ds = (p * (dot(v[c], gs, NT) - final[1, h : h + 1, r])).astype(BF16)
            v_part = dot(p.astype(BF16), gs, NN)
            k_part = dot(ds, qs, NN)
            for n, j in enumerate(reach):
                rj = slice(j * BLOCK, (j + 1) * BLOCK)
                here = slice(n * BLOCK, (n + 1) * BLOCK)
                if h == 0 and b == near(j, blocks)[0]:
                    dv[rj] = v_part[here]
                    dk[rj] = k_part[here]
                else:
                    dv[rj] += v_part[here]
                    dk[rj] += k_part[here]
            dq_t[hr, r] = part[hr, r] + dot(k_t[hr, c], ds, NN)
    dq[...] = dq_t[...].T.astype(BF16)


def local(q, k, v, g, part, final, before, width, depth, scale, pair):
    rows, cols = q.shape
    hp = width // depth
    column = pl.BlockSpec((rows, width), lambda i: (0, pair))
    alone = pl.BlockSpec((rows, width), lambda i: (0, 0))
    extra = [] if before is None else [before]
    return call(
        functools.partial(local_body, depth, scale, len(extra)),
        flops=10 * 3 * BLOCK * rows * width,
        moved=rows * width * 24,
        grid=(1,),
        in_specs=[column] * 4
        + [
            pl.BlockSpec((width, rows), lambda i: (pair, 0)),
            pl.BlockSpec((None, 2, hp, rows), lambda i: (pair, 0, 0, 0)),
        ]
        + [ANY] * len(extra),
        out_specs=[column, alone, alone],
        out_shape=[struct((rows, cols), BF16)] + [struct((rows, width), F32)] * 2,
        scratch_shapes=[pltpu.VMEM((width, rows), BF16), pltpu.VMEM((width, rows), F32)],
        input_output_aliases={6: 0} if extra else {},
    )(q, k, v, g, part, final, *extra)


def gathered(kept, got, n):
    rows = kept.shape[1]
    total = kept[n]
    for part in got:
        at = rows - part.shape[1]
        more = part[n].astype(F32)
        if at:
            more = jnp.concatenate([jnp.zeros((at, more.shape[1]), F32), more], axis=0)
        total = total + more
    return total


def fold(kept, got, cuts, tokens=(), passed=()):
    cols = kept.shape[-1]
    vmem = pl.BlockSpec(memory_space=pltpu.VMEM)
    extra = list(passed) + list(tokens)
    count = len(got)
    sizes = [b - a for a, b in zip(cuts, cuts[1:])]

    def body(kept, *rest):
        arrived = rest[:count]
        outs = rest[count + len(extra) :]
        for n in range(2):
            total = gathered(kept, arrived, n)
            outs[0][n] = total[: cuts[0]]
            for a, b, out in zip(cuts, cuts[1:], outs[1:]):
                out[n] = total[a:b].astype(BF16)

    return call(
        body,
        moved=kept.size * 8,
        in_specs=[vmem] * (1 + count) + [ANY] * len(extra),
        out_specs=[vmem] * len(cuts) + [ANY] * len(passed),
        out_shape=[struct((2, cuts[0], cols), F32)]
        + [struct((2, size, cols), BF16) for size in sizes]
        + [struct(x.shape, x.dtype) for x in passed],
        input_output_aliases={1 + count + n: len(cuts) + n for n in range(len(passed))},
    )(kept, *got, *extra)


def finish_body(pairs, ends, *refs):
    dk, dv = refs[:pairs], refs[pairs : 2 * pairs]
    from_inner, from_outer, wide_group, wide_whole, kept = refs[2 * pairs : 2 * pairs + 5]
    got, (out_k, out_v) = refs[2 * pairs + 5 : -2], refs[-2:]
    block = pl.program_id(0)
    blocks = pl.num_programs(0)
    width = dk[0].shape[1]
    per = BLOCK // SEG1
    rows = kept.shape[1]
    count1 = rows * SEG2 // (SEG1 + SEG2)
    odd = ends[2]
    from_in = jnp.where(block == (1 - odd) * (blocks - 1), 1.0, 0.0)
    from_out = jnp.where(block == odd * (blocks - 1), 1.0, 0.0)
    index = lax.broadcasted_iota(jnp.int32, (rows, 1), 0)
    for n, (src, dst) in enumerate(((dk, out_k), (dv, out_v))):
        sums = gathered(kept, got, n)
        whole = jnp.sum(jnp.where(index == count1 + block, sums, 0.0), axis=0, keepdims=True)
        for s in range(per):
            mine = jnp.where(index == block * per + s, sums, 0.0)
            group = jnp.sum(mine, axis=0, keepdims=True)
            c = slice(s * SEG1, (s + 1) * SEG1)
            piece = group * wide_group[...] + whole * wide_whole[c]
            piece = piece + from_in * from_inner[n, c].astype(F32)
            piece = piece + from_out * from_outer[n, c].astype(F32)
            for p in range(pairs):
                lanes = slice(p * width, (p + 1) * width)
                dst[c, lanes] = (piece[:, lanes] + src[p][c]).astype(BF16)


def finish(dk, dv, from_inner, from_outer, kept, got, wide_group, wide_whole, ends):
    rows, width = dk[0].shape
    pairs = len(dk)
    cols = width * pairs
    tile = pl.BlockSpec((BLOCK, cols), lambda i, *_: (i, 0))
    narrow = pl.BlockSpec((BLOCK, width), lambda i, *_: (i, 0))
    full = lambda x: pl.BlockSpec(x.shape, lambda i, *_: (0,) * x.ndim)
    fixed = [from_inner, from_outer, wide_group, wide_whole, kept] + list(got)
    return call(
        functools.partial(finish_body, pairs),
        moved=rows * cols * 12,
        grid_spec=pltpu.PrefetchScalarGridSpec(
            num_scalar_prefetch=1,
            grid=(rows // BLOCK,),
            in_specs=[narrow] * (2 * pairs) + [full(x) for x in fixed],
            out_specs=[tile, tile],
        ),
        out_shape=[struct((rows, cols), BF16)] * 2,
    )(ends, *dk, *dv, *fixed)


def shards(query, key, value, out_grad, pool_group, pool_global):
    rows, cols = query.shape
    heads = pool_group.shape[0]
    depth = cols // heads
    scale = 1.0 / math.sqrt(depth)
    width = 128 if cols % 128 == 0 and 128 % depth == 0 else cols
    pairs = cols // width
    devices = lax.axis_size("seq")
    position = lax.axis_index("seq")
    count1 = rows // SEG1
    group_bits = list(range(1, GROUP.bit_length() - 1))
    other_bits = list(range(GROUP.bit_length() - 1, devices.bit_length() - 1))

    def swap(array, *bits):
        mask = sum(1 << bit for bit in bits)
        return lax.ppermute(array, "seq", [(i, i ^ mask) for i in range(devices)])

    def cross(array):
        route = [(i, i + 1) for i in range(1, devices - 1, 2)]
        return lax.ppermute(array, "seq", route + [(b, a) for a, b in route])

    ends = jnp.stack([position == 0, position == devices - 1, position % 2 == 1])
    ends = ends.astype(jnp.int32)
    groups, wholes, inner, outer, wide_group, wide_whole = pool(
        key, value, pool_group, pool_global, ends, width
    )
    partial = [
        stats(query, key, value, out_grad, width, depth, scale, p) for p in range(pairs)
    ]
    waiting = list(partial)

    def token():
        return [waiting.pop(0)] if waiting else []

    for bit in other_bits[:-1]:
        got = swap(wholes, bit)
        wholes = join([[wholes, got]])[0][0]
    base, far_bit = group_bits[0], other_bits[-1:]
    (pair,) = join([[groups, wholes]])
    here, there = [groups, wholes], []
    there = [swap(pair[0], base)]
    for bit in far_bit:
        here.append(swap(wholes, bit))
        there.append(swap(wholes, base, bit))
    comb, outer, inner = join([here, there], token(), [outer, inner])
    for bit in group_bits[1:]:
        got = swap(comb, bit)
        (comb,) = join([comb, got], token())
    theirs = swap(comb, 0)
    outer = cross(outer)
    inner = swap(inner, 0)

    kept, sent, inner_d, outer_d, dq_t, final = remote(
        query, out_grad, inner, outer, comb, theirs, partial, ends, width, depth, scale
    )
    got = [swap(sent, 0)]

    query_grad, dk, dv = None, [], []

    def step():
        nonlocal query_grad
        if len(dk) == pairs:
            return []
        query_grad, a, b = local(
            query, key, value, out_grad, dq_t, final, query_grad, width, depth, scale, len(dk)
        )
        dk.append(a)
        dv.append(b)
        return [a]

    from_inner = from_outer = None
    for bit in reversed(group_bits[1:]):
        size = kept.shape[1]
        if from_outer is None:
            kept, sent, inner_d, outer_d = fold(
                kept, got, [size // 2, size], step(), [inner_d, outer_d]
            )
            got = [swap(sent, bit)]
            from_outer = cross(outer_d)
            from_inner = swap(inner_d, 0)
        else:
            kept, sent = fold(kept, got, [size // 2, size], step())
            got = [swap(sent, bit)]
    slot = kept.shape[1] // 2
    own = slot - (slot - count1) // 2 if far_bit else slot
    last = []
    while len(dk) < pairs - 1:
        last = step()
    if far_bit:
        kept, far_here, to_base, far_there = fold(kept, got, [own, slot, slot + own, 2 * slot], last)
        got = [swap(to_base, base), swap(far_here, far_bit[0]), swap(far_there, base, far_bit[0])]
    else:
        kept, to_base = fold(kept, got, [slot, 2 * slot], last)
        got = [swap(to_base, base)]
    for bit in reversed(other_bits[:-1]):
        size = kept.shape[1]
        cut = count1 + (size - count1) // 2
        kept, sent = fold(kept, got, [cut, size])
        got = [swap(sent, bit)]
    while len(dk) < pairs:
        step()
    key_grad, value_grad = finish(
        dk, dv, from_inner, from_outer, kept, got, wide_group, wide_whole, ends
    )
    return (query_grad, key_grad, value_grad)


def solution(mesh):
    rows = P("seq", "head")
    in_specs = (rows, rows, rows, rows, P("head", None), P("head", None))
    return jax.shard_map(
        shards, mesh=mesh, in_specs=in_specs, out_specs=(rows, rows, rows), check_vma=False
    )
```

```python
import functools
import math

import jax
import jax.numpy as jnp
from jax import lax
from jax.experimental import pallas as pl
from jax.experimental.pallas import tpu as pltpu
from jax.sharding import PartitionSpec as P


BLOCK = 256
SEG1 = 64
SEG2 = 256
GROUP = 8
NEG = -1e30
F32 = jnp.float32
BF16 = jnp.bfloat16
NT = (((1,), (1,)), ((), ()))
NN = (((1,), (0,)), ((), ()))
VMEM_LIMIT = 32 * 2**20
ANY = pl.BlockSpec(memory_space=pl.ANY)


def dot(a, b, dims):
    return lax.dot_general(a, b, dims, preferred_element_type=F32)


def struct(shape, dtype):
    return jax.ShapeDtypeStruct(shape, dtype)


def call(body, flops=0, moved=0, vmem=VMEM_LIMIT, **kwargs):
    cost = pl.CostEstimate(flops=int(flops), bytes_accessed=int(moved), transcendentals=0)
    params = pltpu.CompilerParams(vmem_limit_bytes=vmem)
    return pl.pallas_call(body, cost_estimate=cost, compiler_params=params, **kwargs)


def head_masks(width, depth):
    lane = lax.broadcasted_iota(jnp.int32, (1, width), 1)
    return [(lane >= h * depth) & (lane < (h + 1) * depth) for h in range(width // depth)]


def keep_head(rows, mask, scale=None):
    rows = jnp.where(mask, rows, 0)
    if scale is not None:
        rows = rows.astype(F32) * scale
    return rows.astype(BF16)


def near(block, blocks):
    return range(max(block - 1, 0), min(block + 2, blocks))


def is_odd():
    return lax.rem(lax.axis_index("seq"), 2)


def pool_body(depth, k, v, group_pool, whole_pool, groups, wholes, inner, outer, *rest):
    *bufs, group_w, whole_w, sems = rest
    rows, cols = bufs[0].shape
    heads = group_w.shape[0]
    chunks = rows // SEG2
    copies = [
        pltpu.make_async_copy(group_pool, group_w, sems.at[2 * chunks]),
        pltpu.make_async_copy(whole_pool, whole_w, sems.at[2 * chunks + 1]),
    ]
    for c in range(chunks):
        r = pl.ds(c * SEG2, SEG2)
        for n, src in enumerate((k, v)):
            copies.append(pltpu.make_async_copy(src.at[r], bufs[n].at[r], sems.at[2 * c + n]))
    for copy in copies:
        copy.start()
    copies[0].wait()
    copies[1].wait()
    per = SEG2 // SEG1
    lane = lax.broadcasted_iota(jnp.int32, (heads, SEG2), 1)
    tiled = jnp.concatenate([group_w[...]] * per, axis=1)
    weights = [
        jnp.where((lane >= s * SEG1) & (lane < (s + 1) * SEG1), tiled, 0.0) for s in range(per)
    ]
    rest = jnp.concatenate(weights + [whole_w[...]], axis=0)
    terms = []
    for _ in range(3):
        term = rest.astype(BF16)
        terms.append(term)
        rest = rest - term.astype(F32)
    left = jnp.concatenate(terms, axis=0)
    size = (per + 1) * heads
    head = lax.broadcasted_iota(jnp.int32, (heads, cols), 0)
    col = lax.broadcasted_iota(jnp.int32, (heads, cols), 1)
    pick = (col >= head * depth) & (col < (head + 1) * depth)
    sums = [([], []), ([], [])]
    for c in range(chunks):
        for n in range(2):
            copies[2 + 2 * c + n].wait()
            full = dot(left, bufs[n][c * SEG2 : (c + 1) * SEG2], NN)
            full = full[:size] + full[size : 2 * size] + full[2 * size :]
            for s in range(per + 1):
                mine = jnp.where(pick, full[s * heads : (s + 1) * heads], 0.0)
                sums[n][s == per].append(jnp.sum(mine, axis=0, keepdims=True))
    odd = is_odd()
    low = pl.multiple_of(odd * (rows - BLOCK), BLOCK)
    high = pl.multiple_of((1 - odd) * (rows - BLOCK), BLOCK)
    for n in range(2):
        groups[n] = jnp.concatenate(sums[n][0], axis=0).astype(BF16)
        wholes[n] = jnp.concatenate(sums[n][1], axis=0).astype(BF16)
        inner[n] = bufs[n][pl.ds(high, BLOCK)]
        outer[n] = bufs[n][pl.ds(low, BLOCK)]


def pool(k, v, group_pool, whole_pool):
    rows, cols = k.shape
    heads = group_pool.shape[0]
    count1, count2 = rows // SEG1, rows // SEG2
    shapes = [(2, count1, cols), (2, count2, cols), (2, BLOCK, cols), (2, BLOCK, cols)]
    shapes += [k.shape, v.shape]
    inputs = [
        pltpu.with_memory_space_constraint(x, pltpu.HBM) for x in (k, v, group_pool, whole_pool)
    ]
    return call(
        functools.partial(pool_body, cols // heads),
        moved=k.size * 6,
        vmem=16 * 2**20,
        in_specs=[pl.BlockSpec(memory_space=pltpu.HBM)] * 4,
        out_specs=[pl.BlockSpec(memory_space=pltpu.VMEM)] * len(shapes),
        out_shape=[struct(shape, BF16) for shape in shapes],
        scratch_shapes=[
            pltpu.VMEM(group_pool.shape, F32),
            pltpu.VMEM(whole_pool.shape, F32),
            pltpu.SemaphoreType.DMA((2 * count2 + 2,)),
        ],
    )(*inputs)


def join(slots, tokens=(), passed=()):
    flat, plan, count, rows = [], [], 0, 0
    for slot in slots:
        if isinstance(slot, list):
            plan.append((count, len(slot)))
            flat += slot
            rows = sum(part.shape[1] for part in slot)
            count += 1
        else:
            plan.append((count, 0))
            flat.append(slot)
            rows = slot.shape[2]
            count += slot.shape[0]
    cols = flat[0].shape[-1]
    extra = list(passed) + list(tokens)

    def body(*refs):
        out = refs[len(flat) + len(extra)]
        at = 0
        for start, parts in plan:
            if not parts:
                out[start : start + refs[at].shape[0]] = refs[at][...]
                at += 1
                continue
            for n in range(2):
                pieces = [refs[at + i][n].astype(F32) for i in range(parts)]
                out[start, n] = jnp.concatenate(pieces, axis=0).astype(BF16)
            at += parts

    vmem = pl.BlockSpec(memory_space=pltpu.VMEM)
    return call(
        body,
        moved=4 * count * 2 * rows * cols,
        in_specs=[vmem] * len(flat) + [ANY] * len(extra),
        out_specs=[vmem] + [ANY] * len(passed),
        out_shape=[struct((count, 2, rows, cols), BF16)]
        + [struct(x.shape, x.dtype) for x in passed],
        input_output_aliases={len(flat) + n: 1 + n for n in range(len(passed))},
    )(*flat, *extra)


def merge(state, s_all, d_all, chunk=64):
    for c in range(0, s_all.shape[0], chunk):
        s = s_all[c : c + chunk]
        count = s.shape[0] // 8
        s = s.reshape(count, 8, s.shape[1])
        d = d_all[c : c + chunk].reshape(s.shape)
        here = jnp.max(s, axis=0)
        top = here if state is None else jnp.maximum(state[0], here)
        e = jnp.exp(s - top[None])
        total = jnp.sum(e, axis=0)
        inner = jnp.sum(e * d, axis=0)
        if state is not None:
            fade = jnp.exp(state[0] - top)
            total = total + state[1] * fade
            inner = inner + state[2] * fade
        state = (top, total, inner)
    return state


def stats_body(depth, scale, q, k, v, g, out):
    rows, width = q.shape
    blocks = rows // BLOCK
    for h, mask in enumerate(head_masks(width, depth)):
        for b in range(blocks):
            r = slice(b * BLOCK, (b + 1) * BLOCK)
            qs = keep_head(q[r], mask, scale)
            gs = keep_head(g[r], mask)
            c = slice(near(b, blocks)[0] * BLOCK, (near(b, blocks)[-1] + 1) * BLOCK)
            top, total, inner = merge(None, dot(k[c], qs, NT), dot(v[c], gs, NT))
            most = jnp.max(top, axis=0, keepdims=True)
            fade = jnp.exp(top - most)
            out[0, h : h + 1, r] = most
            out[1, h : h + 1, r] = jnp.sum(total * fade, axis=0, keepdims=True)
            out[2, h : h + 1, r] = jnp.sum(inner * fade, axis=0, keepdims=True)


def stats(q, k, v, g, width, depth, scale, pair):
    rows = q.shape[0]
    hp = width // depth
    cols = pl.BlockSpec((rows, width), lambda i: (0, pair))
    return call(
        functools.partial(stats_body, depth, scale),
        flops=2 * 2 * 3 * BLOCK * rows * width,
        moved=rows * width * 8,
        grid=(1,),
        in_specs=[cols] * 4,
        out_specs=pl.BlockSpec((3, hp, rows), lambda i: (0, 0, 0)),
        out_shape=struct((3, hp, rows), F32),
    )(q, k, v, g)


def far_body(depth, scale, pairs, q, g, mine, theirs, *rest):
    partial = rest[:pairs]
    far_k, far_v, out = rest[pairs:]
    rows, width = q.shape
    slots, _, per, _ = mine.shape
    half = slots * per
    pair = pl.program_id(0)
    for n, far in enumerate((far_k, far_v)):
        for m, src in enumerate((mine, theirs)):
            for s in range(slots):
                at = m * half + s * per
                far[at : at + per] = src[s, n]
    for h, mask in enumerate(head_masks(width, depth)):
        for b in range(rows // BLOCK):
            r = slice(b * BLOCK, (b + 1) * BLOCK)
            qs = keep_head(q[r], mask, scale)
            gs = keep_head(g[r], mask)
            old = [partial[0][m, h : h + 1, r] for m in range(3)]
            for n in range(1, pairs):
                old = [
                    jnp.where(pair == n, partial[n][m, h : h + 1, r], old[m]) for m in range(3)
                ]
            state = merge(None, dot(far_k[...], qs, NT), dot(far_v[...], gs, NT))
            for m, value in enumerate(settle(old, state)):
                out[m, h : h + 1, r] = value


def settle(old, state):
    top8, total8, inner8 = state
    top = jnp.maximum(old[0], jnp.max(top8, axis=0, keepdims=True))
    fade = jnp.exp(old[0] - top)
    fade8 = jnp.exp(top8 - top)
    total = old[1] * fade + jnp.sum(total8 * fade8, axis=0, keepdims=True)
    dots = old[2] * fade + jnp.sum(inner8 * fade8, axis=0, keepdims=True)
    return top, total, dots


def far_stats(q, g, mine, theirs, partial, width, depth, scale):
    rows, cols = q.shape
    pairs = cols // width
    hp = width // depth
    slots, _, per, _ = mine.shape
    far = 2 * slots * per
    wide = lambda n: pl.BlockSpec((n, width), lambda i: (0, i))
    slot = pl.BlockSpec((slots, 2, per, width), lambda i: (0, 0, 0, i))
    fixed = pl.BlockSpec((3, hp, rows), lambda i: (0, 0, 0))
    return call(
        functools.partial(far_body, depth, scale, pairs),
        flops=4 * far * rows * cols,
        moved=rows * cols * 4,
        grid=(pairs,),
        in_specs=[wide(rows)] * 2 + [slot] * 2 + [fixed] * pairs,
        out_specs=[wide(far)] * 2 + [pl.BlockSpec((None, 3, hp, rows), lambda i: (i, 0, 0, 0))],
        out_shape=[struct((far, cols), BF16)] * 2 + [struct((pairs, 3, hp, rows), F32)],
    )(q, g, mine, theirs, *partial)


def remote_body(depth, scale, q, g, inner, outer, far_k, far_v, known, *rest):
    kept, sent, inner_d, outer_d, dq_t, final = rest[:6]
    far_kt, near_t, near_d, qs, gs = rest[6:]
    rows, width = q.shape
    blocks = rows // BLOCK
    half = far_k.shape[0] // 2
    masks = head_masks(width, depth)
    far_kt[...] = (far_k[...].astype(F32) * scale).astype(BF16).T
    near_t[0] = (inner[0].astype(F32) * scale).astype(BF16).T
    near_t[1] = (outer[0].astype(F32) * scale).astype(BF16).T
    scaled = (q[...].astype(F32) * scale).astype(BF16)
    for h, mask in enumerate(masks):
        qs[h] = jnp.where(mask, scaled, 0).astype(BF16)
        gs[h] = jnp.where(mask, g[...], 0).astype(BF16)
    odd = is_odd()
    position = lax.axis_index("seq")
    ends = (position == 0) | (position == lax.axis_size("seq") - 1)
    missing = jnp.where(ends, NEG, 0.0)
    places = [
        pl.ds(pl.multiple_of(n * ((blocks - 1) * BLOCK), BLOCK), BLOCK) for n in (1 - odd, odd)
    ]
    halos = ((inner, None), (outer, missing))
    final[0] = known[0] + jnp.log(known[1])
    final[1] = known[2] / known[1]
    for h in range(len(masks)):
        old = None
        for (halo, bias), r in zip(halos, places):
            if old is None or blocks > 1:
                old = [known[m, h : h + 1, r] for m in range(3)]
            s = dot(halo[0], qs[h, r], NT)
            if bias is not None:
                s = s + bias
            old = settle(old, merge(None, s, dot(halo[1], gs[h, r], NT)))
            final[0, h : h + 1, r] = old[0] + jnp.log(old[1])
            final[1, h : h + 1, r] = old[2] / old[1]
    totals = [None, None]
    for h in range(len(masks)):
        hr = slice(h * depth, (h + 1) * depth)
        p = jnp.exp(dot(far_k[...], qs[h], NT) - final[0, h : h + 1, :])
        ds = (p * (dot(far_v[...], gs[h], NT) - final[1, h : h + 1, :])).astype(BF16)
        parts = (dot(ds, qs[h], NN), dot(p.astype(BF16), gs[h], NN))
        totals = [new if old is None else old + new for old, new in zip(totals, parts)]
        dq_t[hr] = dot(far_kt[hr], ds, NN)
        for n, ((halo, bias), r) in enumerate(zip(halos, places)):
            s = dot(halo[0], qs[h, r], NT)
            if bias is not None:
                s = s + bias
            p = jnp.exp(s - final[0, h : h + 1, r])
            ds = (p * (dot(halo[1], gs[h, r], NT) - final[1, h : h + 1, r])).astype(BF16)
            parts = (dot(ds, qs[h, r], NN), dot(p.astype(BF16), gs[h, r], NN))
            for m, part in enumerate(parts):
                if h == 0:
                    near_d[2 * n + m] = part
                else:
                    near_d[2 * n + m] += part
            dq_t[hr, r] += dot(near_t[n, hr], ds, NN)
    for n in range(2):
        kept[n] = totals[n][:half]
        sent[n] = totals[n][half:].astype(BF16)
        inner_d[n] = near_d[n].astype(BF16)
        outer_d[n] = near_d[2 + n].astype(BF16)


def remote(q, g, inner, outer, far_k, far_v, known, width, depth, scale):
    rows, cols = q.shape
    pairs = cols // width
    hp = width // depth
    far = far_k.shape[0]
    half = far // 2
    wide = lambda n: pl.BlockSpec((n, width), lambda i: (0, i))
    both = lambda n: pl.BlockSpec((2, n, width), lambda i: (0, 0, i))
    row = lambda n: pl.BlockSpec((None, n, hp, rows), lambda i: (i, 0, 0, 0))
    return call(
        functools.partial(remote_body, depth, scale),
        flops=10 * (far * rows + 2 * BLOCK * BLOCK) * cols,
        moved=rows * cols * 8,
        grid=(pairs,),
        in_specs=[wide(rows)] * 2 + [both(BLOCK)] * 2 + [wide(far)] * 2 + [row(3)],
        out_specs=[
            both(half),
            both(half),
            both(BLOCK),
            both(BLOCK),
            pl.BlockSpec((width, rows), lambda i: (i, 0)),
            row(2),
        ],
        scratch_shapes=[
            pltpu.VMEM((width, far), BF16),
            pltpu.VMEM((2, width, BLOCK), BF16),
            pltpu.VMEM((4, BLOCK, width), F32),
            pltpu.VMEM((hp, rows, width), BF16),
            pltpu.VMEM((hp, rows, width), BF16),
        ],
        out_shape=[
            struct((2, half, cols), F32),
            struct((2, half, cols), BF16),
            struct((2, BLOCK, cols), BF16),
            struct((2, BLOCK, cols), BF16),
            struct((cols, rows), F32),
            struct((pairs, 2, hp, rows), F32),
        ],
    )(q, g, inner, outer, far_k, far_v, known)


def local_body(depth, scale, chained, q, k, v, g, part, final, *rest):
    dq, dk, dv, k_t, dq_t = rest[chained:]
    rows, width = q.shape
    blocks = rows // BLOCK
    k_t[...] = (k[...].astype(F32) * scale).astype(BF16).T
    for h, mask in enumerate(head_masks(width, depth)):
        hr = slice(h * depth, (h + 1) * depth)
        for b in range(blocks):
            r = slice(b * BLOCK, (b + 1) * BLOCK)
            qs = keep_head(q[r], mask, scale)
            gs = keep_head(g[r], mask)
            reach = near(b, blocks)
            c = slice(reach[0] * BLOCK, (reach[-1] + 1) * BLOCK)
            p = jnp.exp(dot(k[c], qs, NT) - final[0, h : h + 1, r])
            ds = (p * (dot(v[c], gs, NT) - final[1, h : h + 1, r])).astype(BF16)
            v_part = dot(p.astype(BF16), gs, NN)
            k_part = dot(ds, qs, NN)
            for n, j in enumerate(reach):
                rj = slice(j * BLOCK, (j + 1) * BLOCK)
                here = slice(n * BLOCK, (n + 1) * BLOCK)
                if h == 0 and b == near(j, blocks)[0]:
                    dv[rj] = v_part[here]
                    dk[rj] = k_part[here]
                else:
                    dv[rj] += v_part[here]
                    dk[rj] += k_part[here]
            dq_t[hr, r] = part[hr, r] + dot(k_t[hr, c], ds, NN)
    dq[...] = dq_t[...].T.astype(BF16)


def local(q, k, v, g, part, final, before, width, depth, scale, pair):
    rows, cols = q.shape
    hp = width // depth
    column = pl.BlockSpec((rows, width), lambda i: (0, pair))
    alone = pl.BlockSpec((rows, width), lambda i: (0, 0))
    extra = [] if before is None else [before]
    return call(
        functools.partial(local_body, depth, scale, len(extra)),
        flops=10 * 3 * BLOCK * rows * width,
        moved=rows * width * 24,
        grid=(1,),
        in_specs=[column] * 4
        + [
            pl.BlockSpec((width, rows), lambda i: (pair, 0)),
            pl.BlockSpec((None, 2, hp, rows), lambda i: (pair, 0, 0, 0)),
        ]
        + [ANY] * len(extra),
        out_specs=[column, alone, alone],
        out_shape=[struct((rows, cols), BF16)] + [struct((rows, width), F32)] * 2,
        scratch_shapes=[pltpu.VMEM((width, rows), BF16), pltpu.VMEM((width, rows), F32)],
        input_output_aliases={6: 0} if extra else {},
    )(q, k, v, g, part, final, *extra)


def gathered(kept, got, n):
    rows = kept.shape[1]
    total = kept[n]
    for part in got:
        at = rows - part.shape[1]
        more = part[n].astype(F32)
        if at:
            more = jnp.concatenate([jnp.zeros((at, more.shape[1]), F32), more], axis=0)
        total = total + more
    return total


def fold(kept, got, cuts, tokens=(), passed=()):
    cols = kept.shape[-1]
    vmem = pl.BlockSpec(memory_space=pltpu.VMEM)
    extra = list(passed) + list(tokens)
    count = len(got)
    sizes = [b - a for a, b in zip(cuts, cuts[1:])]

    def body(kept, *rest):
        arrived = rest[:count]
        outs = rest[count + len(extra) :]
        for n in range(2):
            total = gathered(kept, arrived, n)
            outs[0][n] = total[: cuts[0]]
            for a, b, out in zip(cuts, cuts[1:], outs[1:]):
                out[n] = total[a:b].astype(BF16)

    return call(
        body,
        moved=kept.size * 8,
        in_specs=[vmem] * (1 + count) + [ANY] * len(extra),
        out_specs=[vmem] * len(cuts) + [ANY] * len(passed),
        out_shape=[struct((2, cuts[0], cols), F32)]
        + [struct((2, size, cols), BF16) for size in sizes]
        + [struct(x.shape, x.dtype) for x in passed],
        input_output_aliases={1 + count + n: len(cuts) + n for n in range(len(passed))},
    )(kept, *got, *extra)


def finish_body(pairs, depth, *refs):
    dk, dv = refs[:pairs], refs[pairs : 2 * pairs]
    from_inner, from_outer, group_pool, whole_pool, kept = refs[2 * pairs : 2 * pairs + 5]
    got = refs[2 * pairs + 5 : -4]
    out_k, out_v, wide_group, wide_whole = refs[-4:]
    block = pl.program_id(0)
    rows, cols = kept.shape[1:]
    heads = group_pool.shape[0]
    width = dk[0].shape[1]
    per = BLOCK // SEG1
    count1 = rows * SEG2 // (SEG1 + SEG2)
    blocks = count1 // per

    @pl.when(block == 0)
    def _():
        head = lax.broadcasted_iota(jnp.int32, (heads, cols), 0)
        col = lax.broadcasted_iota(jnp.int32, (heads, cols), 1)
        pick = ((col >= head * depth) & (col < (head + 1) * depth)).astype(F32)
        for src, dst in ((group_pool, wide_group), (whole_pool, wide_whole)):
            dst[...] = lax.dot_general(
                src[...],
                pick,
                (((0,), (0,)), ((), ())),
                precision=lax.Precision.HIGHEST,
                preferred_element_type=F32,
            )

    def emit(halos):
        index = lax.broadcasted_iota(jnp.int32, (rows, 1), 0)
        for n, (src, dst) in enumerate(((dk, out_k), (dv, out_v))):
            sums = gathered(kept, got, n)
            whole = jnp.sum(jnp.where(index == count1 + block, sums, 0.0), axis=0, keepdims=True)
            for s in range(per):
                mine = jnp.where(index == block * per + s, sums, 0.0)
                group = jnp.sum(mine, axis=0, keepdims=True)
                c = slice(s * SEG1, (s + 1) * SEG1)
                piece = group * wide_group[...] + whole * wide_whole[c]
                for halo in halos:
                    piece = piece + halo[n, c].astype(F32)
                for p in range(pairs):
                    lanes = slice(p * width, (p + 1) * width)
                    dst[c, lanes] = (piece[:, lanes] + src[p][c]).astype(BF16)

    if blocks == 1:
        emit((from_inner, from_outer))
        return
    odd = is_odd()
    at_inner = block == (1 - odd) * (blocks - 1)
    at_outer = block == odd * (blocks - 1)
    pl.when(at_inner)(lambda: emit((from_inner,)))
    pl.when(at_outer)(lambda: emit((from_outer,)))
    pl.when(jnp.logical_not(at_inner | at_outer))(lambda: emit(()))


def finish(dk, dv, from_inner, from_outer, kept, got, group_pool, whole_pool):
    rows, width = dk[0].shape
    pairs = len(dk)
    cols = width * pairs
    depth = cols // group_pool.shape[0]
    tile = pl.BlockSpec((BLOCK, cols), lambda i: (i, 0))
    narrow = pl.BlockSpec((BLOCK, width), lambda i: (i, 0))
    full = lambda x: pl.BlockSpec(x.shape, lambda i: (0,) * x.ndim)
    fixed = [from_inner, from_outer, group_pool, whole_pool, kept] + list(got)
    return call(
        functools.partial(finish_body, pairs, depth),
        moved=rows * cols * 12,
        grid=(rows // BLOCK,),
        in_specs=[narrow] * (2 * pairs) + [full(x) for x in fixed],
        out_specs=[tile, tile],
        out_shape=[struct((rows, cols), BF16)] * 2,
        scratch_shapes=[pltpu.VMEM((SEG1, cols), F32), pltpu.VMEM((SEG2, cols), F32)],
    )(*dk, *dv, *fixed)


def shards(query, key, value, out_grad, pool_group, pool_global):
    rows, cols = query.shape
    heads = pool_group.shape[0]
    depth = cols // heads
    scale = 1.0 / math.sqrt(depth)
    width = 128 if cols % 128 == 0 and 128 % depth == 0 else cols
    pairs = cols // width
    devices = lax.axis_size("seq")
    count1 = rows // SEG1
    group_bits = list(range(1, GROUP.bit_length() - 1))
    other_bits = list(range(GROUP.bit_length() - 1, devices.bit_length() - 1))

    def swap(array, *bits):
        mask = sum(1 << bit for bit in bits)
        return lax.ppermute(array, "seq", [(i, i ^ mask) for i in range(devices)])

    def cross(array):
        route = [(i, i + 1) for i in range(1, devices - 1, 2)]
        return lax.ppermute(array, "seq", route + [(b, a) for a, b in route])

    groups, wholes, inner, outer, key, value = pool(key, value, pool_group, pool_global)
    partial = [
        stats(query, key, value, out_grad, width, depth, scale, p) for p in range(pairs)
    ]
    waiting = list(partial)

    def token():
        return [waiting.pop(0)] if waiting else []

    for bit in other_bits[:-1]:
        got = swap(wholes, bit)
        wholes = join([[wholes, got]])[0][0]
    base, far_bit = group_bits[0], other_bits[-1:]
    (pair,) = join([[groups, wholes]])
    here, there = [groups, wholes], []
    there = [swap(pair[0], base)]
    for bit in far_bit:
        here.append(swap(wholes, bit))
        there.append(swap(wholes, base, bit))
    comb, outer, inner = join([here, there], token(), [outer, inner])
    for bit in group_bits[1:]:
        got = swap(comb, bit)
        (comb,) = join([comb, got], token())
    theirs = swap(comb, 0)
    outer = cross(outer)
    inner = swap(inner, 0)

    far_k, far_v, known = far_stats(
        query, out_grad, comb, theirs, partial, width, depth, scale
    )
    kept, sent, inner_d, outer_d, dq_t, final = remote(
        query, out_grad, inner, outer, far_k, far_v, known, width, depth, scale
    )
    got = [swap(sent, 0)]

    query_grad, dk, dv = None, [], []

    def step():
        nonlocal query_grad
        if len(dk) == pairs:
            return []
        query_grad, a, b = local(
            query, key, value, out_grad, dq_t, final, query_grad, width, depth, scale, len(dk)
        )
        dk.append(a)
        dv.append(b)
        return [a]

    from_inner = from_outer = None
    for bit in reversed(group_bits[1:]):
        size = kept.shape[1]
        if from_outer is None:
            kept, sent, inner_d, outer_d = fold(
                kept, got, [size // 2, size], step(), [inner_d, outer_d]
            )
            got = [swap(sent, bit)]
            from_outer = cross(outer_d)
            from_inner = swap(inner_d, 0)
        else:
            kept, sent = fold(kept, got, [size // 2, size], step())
            got = [swap(sent, bit)]
    slot = kept.shape[1] // 2
    own = slot - (slot - count1) // 2 if far_bit else slot
    last = []
    while len(dk) < pairs - 1:
        last = step()
    if far_bit:
        kept, far_here, to_base, far_there = fold(kept, got, [own, slot, slot + own, 2 * slot], last)
        got = [swap(to_base, base), swap(far_here, far_bit[0]), swap(far_there, base, far_bit[0])]
    else:
        kept, to_base = fold(kept, got, [slot, 2 * slot], last)
        got = [swap(to_base, base)]
    for bit in reversed(other_bits[:-1]):
        size = kept.shape[1]
        cut = count1 + (size - count1) // 2
        kept, sent = fold(kept, got, [cut, size])
        got = [swap(sent, bit)]
    while len(dk) < pairs:
        step()
    key_grad, value_grad = finish(
        dk, dv, from_inner, from_outer, kept, got, pool_group, pool_global
    )
    return (query_grad, key_grad, value_grad)


def solution(mesh):
    rows = P("seq", "head")
    in_specs = (rows, rows, rows, rows, P("head", None), P("head", None))
    return jax.shard_map(
        shards, mesh=mesh, in_specs=in_specs, out_specs=(rows, rows, rows), check_vma=False
    )
```

```python
import functools
import math

import jax
import jax.numpy as jnp
from jax import lax
from jax.experimental import pallas as pl
from jax.experimental.pallas import tpu as pltpu
from jax.sharding import PartitionSpec as P


BLOCK = 256
SEG1 = 64
SEG2 = 256
GROUP = 8
NEG = -1e30
F32 = jnp.float32
BF16 = jnp.bfloat16
NT = (((1,), (1,)), ((), ()))
NN = (((1,), (0,)), ((), ()))
VMEM_LIMIT = 32 * 2**20
ANY = pl.BlockSpec(memory_space=pl.ANY)
WHOLE = pl.BlockSpec(memory_space=pltpu.VMEM)


def dot(a, b, dims):
    return lax.dot_general(a, b, dims, preferred_element_type=F32)


def struct(shape, dtype):
    return jax.ShapeDtypeStruct(shape, dtype)


def call(body, flops=0, moved=0, vmem=VMEM_LIMIT, **kwargs):
    cost = pl.CostEstimate(flops=int(flops), bytes_accessed=int(moved), transcendentals=0)
    params = pltpu.CompilerParams(vmem_limit_bytes=vmem)
    return pl.pallas_call(body, cost_estimate=cost, compiler_params=params, **kwargs)


def head_masks(width, depth):
    lane = lax.broadcasted_iota(jnp.int32, (1, width), 1)
    return [(lane >= h * depth) & (lane < (h + 1) * depth) for h in range(width // depth)]


def keep_head(rows, mask, scale=None):
    rows = jnp.where(mask, rows, 0)
    if scale is not None:
        rows = rows.astype(F32) * scale
    return rows.astype(BF16)


def near(block, blocks):
    return range(max(block - 1, 0), min(block + 2, blocks))


def is_odd():
    return lax.rem(lax.axis_index("seq"), 2)


def split(x):
    terms = []
    for _ in range(3):
        term = x.astype(BF16)
        terms.append(term)
        x = x - term.astype(F32)
    return terms


def pooling(group_w, whole_w):
    heads = group_w.shape[0]
    per = SEG2 // SEG1
    lane = lax.broadcasted_iota(jnp.int32, (heads, SEG2), 1)
    tiled = jnp.concatenate([group_w] * per, axis=1)
    rows = [
        jnp.where((lane >= s * SEG1) & (lane < (s + 1) * SEG1), tiled, 0.0) for s in range(per)
    ]
    return jnp.concatenate(rows + [whole_w], axis=0)


def head_columns(heads, cols, depth):
    head = lax.broadcasted_iota(jnp.int32, (heads, cols), 0)
    col = lax.broadcasted_iota(jnp.int32, (heads, cols), 1)
    return (col >= head * depth) & (col < (head + 1) * depth)


def pool_body(depth, k, v, group_pool, whole_pool, groups, wholes, inner, outer, *rest):
    *bufs, group_w, whole_w, sems = rest
    rows, cols = bufs[0].shape
    heads = group_w.shape[0]
    chunks = rows // SEG2
    copies = [
        pltpu.make_async_copy(group_pool, group_w, sems.at[2 * chunks]),
        pltpu.make_async_copy(whole_pool, whole_w, sems.at[2 * chunks + 1]),
    ]
    for c in range(chunks):
        r = pl.ds(c * SEG2, SEG2)
        for n, src in enumerate((k, v)):
            copies.append(pltpu.make_async_copy(src.at[r], bufs[n].at[r], sems.at[2 * c + n]))
    for copy in copies:
        copy.start()
    copies[0].wait()
    copies[1].wait()
    per = SEG2 // SEG1
    left = jnp.concatenate(split(pooling(group_w[...], whole_w[...])), axis=0)
    size = (per + 1) * heads
    pick = head_columns(heads, cols, depth)
    sums = [([], []), ([], [])]
    for c in range(chunks):
        for n in range(2):
            copies[2 + 2 * c + n].wait()
            full = dot(left, bufs[n][c * SEG2 : (c + 1) * SEG2], NN)
            full = full[:size] + full[size : 2 * size] + full[2 * size :]
            for s in range(per + 1):
                mine = jnp.where(pick, full[s * heads : (s + 1) * heads], 0.0)
                sums[n][s == per].append(jnp.sum(mine, axis=0, keepdims=True))
    odd = is_odd()
    low = pl.multiple_of(odd * (rows - BLOCK), BLOCK)
    high = pl.multiple_of((1 - odd) * (rows - BLOCK), BLOCK)
    for n in range(2):
        groups[n] = jnp.concatenate(sums[n][0], axis=0).astype(BF16)
        wholes[n] = jnp.concatenate(sums[n][1], axis=0).astype(BF16)
        inner[n] = bufs[n][pl.ds(high, BLOCK)]
        outer[n] = bufs[n][pl.ds(low, BLOCK)]


def pool(k, v, group_pool, whole_pool):
    rows, cols = k.shape
    heads = group_pool.shape[0]
    count1, count2 = rows // SEG1, rows // SEG2
    shapes = [(2, count1, cols), (2, count2, cols), (2, BLOCK, cols), (2, BLOCK, cols)]
    shapes += [k.shape, v.shape]
    inputs = [
        pltpu.with_memory_space_constraint(x, pltpu.HBM) for x in (k, v, group_pool, whole_pool)
    ]
    return call(
        functools.partial(pool_body, cols // heads),
        moved=k.size * 6,
        vmem=16 * 2**20,
        in_specs=[pl.BlockSpec(memory_space=pltpu.HBM)] * 4,
        out_specs=[pl.BlockSpec(memory_space=pltpu.VMEM)] * len(shapes),
        out_shape=[struct(shape, BF16) for shape in shapes],
        scratch_shapes=[
            pltpu.VMEM(group_pool.shape, F32),
            pltpu.VMEM(whole_pool.shape, F32),
            pltpu.SemaphoreType.DMA((2 * count2 + 2,)),
        ],
    )(*inputs)


def join(slots, tokens=(), passed=()):
    flat, plan, count, rows = [], [], 0, 0
    for slot in slots:
        if isinstance(slot, list):
            plan.append((count, len(slot)))
            flat += slot
            rows = sum(part.shape[1] for part in slot)
            count += 1
        else:
            plan.append((count, 0))
            flat.append(slot)
            rows = slot.shape[2]
            count += slot.shape[0]
    cols = flat[0].shape[-1]
    extra = list(passed) + list(tokens)

    def body(*refs):
        out = refs[len(flat) + len(extra)]
        at = 0
        for start, parts in plan:
            if not parts:
                out[start : start + refs[at].shape[0]] = refs[at][...]
                at += 1
                continue
            for n in range(2):
                pieces = [refs[at + i][n].astype(F32) for i in range(parts)]
                out[start, n] = jnp.concatenate(pieces, axis=0).astype(BF16)
            at += parts

    vmem = pl.BlockSpec(memory_space=pltpu.VMEM)
    return call(
        body,
        moved=4 * count * 2 * rows * cols,
        in_specs=[vmem] * len(flat) + [ANY] * len(extra),
        out_specs=[vmem] + [ANY] * len(passed),
        out_shape=[struct((count, 2, rows, cols), BF16)]
        + [struct(x.shape, x.dtype) for x in passed],
        input_output_aliases={len(flat) + n: 1 + n for n in range(len(passed))},
    )(*flat, *extra)


def merge(state, s_all, d_all, chunk=64):
    for c in range(0, s_all.shape[0], chunk):
        s = s_all[c : c + chunk]
        count = s.shape[0] // 8
        s = s.reshape(count, 8, s.shape[1])
        d = d_all[c : c + chunk].reshape(s.shape)
        here = jnp.max(s, axis=0)
        top = here if state is None else jnp.maximum(state[0], here)
        e = jnp.exp(s - top[None])
        total = jnp.sum(e, axis=0)
        inner = jnp.sum(e * d, axis=0)
        if state is not None:
            fade = jnp.exp(state[0] - top)
            total = total + state[1] * fade
            inner = inner + state[2] * fade
        state = (top, total, inner)
    return state


def stats_body(depth, scale, width, pair, *refs):
    lanes = slice(pair * width, (pair + 1) * width)
    q, k, v, g = (ref.at[:, lanes] for ref in refs[:4])
    out = refs[4]
    rows = q.shape[0]
    blocks = rows // BLOCK
    for h, mask in enumerate(head_masks(width, depth)):
        for b in range(blocks):
            r = slice(b * BLOCK, (b + 1) * BLOCK)
            qs = keep_head(q[r], mask, scale)
            gs = keep_head(g[r], mask)
            c = slice(near(b, blocks)[0] * BLOCK, (near(b, blocks)[-1] + 1) * BLOCK)
            top, total, inner = merge(None, dot(k[c], qs, NT), dot(v[c], gs, NT))
            most = jnp.max(top, axis=0, keepdims=True)
            fade = jnp.exp(top - most)
            out[0, h : h + 1, r] = most
            out[1, h : h + 1, r] = jnp.sum(total * fade, axis=0, keepdims=True)
            out[2, h : h + 1, r] = jnp.sum(inner * fade, axis=0, keepdims=True)


def stats(q, k, v, g, width, depth, scale, pair):
    rows = q.shape[0]
    hp = width // depth
    return call(
        functools.partial(stats_body, depth, scale, width, pair),
        flops=2 * 2 * 3 * BLOCK * rows * width,
        moved=rows * width * 8,
        in_specs=[WHOLE] * 4,
        out_specs=WHOLE,
        out_shape=struct((3, hp, rows), F32),
    )(q, k, v, g)


def far_body(depth, scale, width, pairs, q, g, mine, theirs, *rest):
    partial = rest[:pairs]
    far_k, far_v, known = rest[pairs:]
    rows = q.shape[0]
    slots, _, per, _ = mine.shape
    half = slots * per
    pair = pl.program_id(0)
    lanes = pl.ds(pl.multiple_of(pair * width, width), width)
    q, g, far_k, far_v = (ref.at[:, lanes] for ref in (q, g, far_k, far_v))
    mine, theirs = (ref.at[:, :, :, lanes] for ref in (mine, theirs))
    out = known.at[pair]
    for n, far in enumerate((far_k, far_v)):
        for m, src in enumerate((mine, theirs)):
            for s in range(slots):
                at = m * half + s * per
                far[at : at + per] = src[s, n]
    for h, mask in enumerate(head_masks(width, depth)):
        for b in range(rows // BLOCK):
            r = slice(b * BLOCK, (b + 1) * BLOCK)
            qs = keep_head(q[r], mask, scale)
            gs = keep_head(g[r], mask)
            old = [partial[0][m, h : h + 1, r] for m in range(3)]
            for n in range(1, pairs):
                old = [
                    jnp.where(pair == n, partial[n][m, h : h + 1, r], old[m]) for m in range(3)
                ]
            state = merge(None, dot(far_k[...], qs, NT), dot(far_v[...], gs, NT))
            for m, value in enumerate(settle(old, state)):
                out[m, h : h + 1, r] = value


def settle(old, state):
    top8, total8, inner8 = state
    top = jnp.maximum(old[0], jnp.max(top8, axis=0, keepdims=True))
    fade = jnp.exp(old[0] - top)
    fade8 = jnp.exp(top8 - top)
    total = old[1] * fade + jnp.sum(total8 * fade8, axis=0, keepdims=True)
    dots = old[2] * fade + jnp.sum(inner8 * fade8, axis=0, keepdims=True)
    return top, total, dots


def far_stats(q, g, mine, theirs, partial, width, depth, scale):
    rows, cols = q.shape
    pairs = cols // width
    hp = width // depth
    slots, _, per, _ = mine.shape
    far = 2 * slots * per
    return call(
        functools.partial(far_body, depth, scale, width, pairs),
        flops=4 * far * rows * cols,
        moved=rows * cols * 4,
        grid=(pairs,),
        in_specs=[WHOLE] * (4 + pairs),
        out_specs=[WHOLE] * 3,
        out_shape=[struct((far, cols), BF16)] * 2 + [struct((pairs, 3, hp, rows), F32)],
    )(q, g, mine, theirs, *partial)


def remote_body(depth, scale, width, q, g, inner, outer, far_k, far_v, known, *rest):
    far_kt, near_t, near_d, qs, gs, s_held, d_held = rest[6:]
    rows = q.shape[0]
    blocks = rows // BLOCK
    half = far_k.shape[0] // 2
    masks = head_masks(width, depth)
    pair = pl.program_id(0)
    lanes = pl.ds(pl.multiple_of(pair * width, width), width)
    q, g, far_k, far_v = (ref.at[:, lanes] for ref in (q, g, far_k, far_v))
    inner, outer = (ref.at[:, :, lanes] for ref in (inner, outer))
    kept, sent, inner_d, outer_d = (ref.at[:, :, lanes] for ref in rest[:4])
    dq_t = rest[4].at[lanes]
    final = rest[5].at[pair]
    known = known.at[pair]
    far_kt[...] = (far_k[...].astype(F32) * scale).astype(BF16).T
    near_t[0] = (inner[0].astype(F32) * scale).astype(BF16).T
    near_t[1] = (outer[0].astype(F32) * scale).astype(BF16).T
    scaled = (q[...].astype(F32) * scale).astype(BF16)
    for h, mask in enumerate(masks):
        qs[h] = jnp.where(mask, scaled, 0).astype(BF16)
        gs[h] = jnp.where(mask, g[...], 0).astype(BF16)
    odd = is_odd()
    position = lax.axis_index("seq")
    ends = (position == 0) | (position == lax.axis_size("seq") - 1)
    missing = jnp.where(ends, NEG, 0.0)
    places = [
        pl.ds(pl.multiple_of(n * ((blocks - 1) * BLOCK), BLOCK), BLOCK) for n in (1 - odd, odd)
    ]
    halos = ((inner, None), (outer, missing))
    final[0] = known[0] + jnp.log(known[1])
    final[1] = known[2] / known[1]
    for h in range(len(masks)):
        old = None
        for n, ((halo, bias), r) in enumerate(zip(halos, places)):
            if old is None or blocks > 1:
                old = [known[m, h : h + 1, r] for m in range(3)]
            s = dot(halo[0], qs[h, r], NT)
            if bias is not None:
                s = s + bias
            d = dot(halo[1], gs[h, r], NT)
            s_held[2 * h + n] = s
            d_held[2 * h + n] = d
            old = settle(old, merge(None, s, d))
            final[0, h : h + 1, r] = old[0] + jnp.log(old[1])
            final[1, h : h + 1, r] = old[2] / old[1]
    totals = [None, None]
    for h in range(len(masks)):
        hr = slice(h * depth, (h + 1) * depth)
        p = jnp.exp(dot(far_k[...], qs[h], NT) - final[0, h : h + 1, :])
        ds = (p * (dot(far_v[...], gs[h], NT) - final[1, h : h + 1, :])).astype(BF16)
        parts = (dot(ds, qs[h], NN), dot(p.astype(BF16), gs[h], NN))
        totals = [new if old is None else old + new for old, new in zip(totals, parts)]
        dq_t[hr] = dot(far_kt[hr], ds, NN)
        for n, r in enumerate(places):
            p = jnp.exp(s_held[2 * h + n] - final[0, h : h + 1, r])
            ds = (p * (d_held[2 * h + n] - final[1, h : h + 1, r])).astype(BF16)
            parts = (dot(ds, qs[h, r], NN), dot(p.astype(BF16), gs[h, r], NN))
            for m, part in enumerate(parts):
                if h == 0:
                    near_d[2 * n + m] = part
                else:
                    near_d[2 * n + m] += part
            dq_t[hr, r] += dot(near_t[n, hr], ds, NN)
    for n in range(2):
        kept[n] = totals[n][:half]
        sent[n] = totals[n][half:].astype(BF16)
        inner_d[n] = near_d[n].astype(BF16)
        outer_d[n] = near_d[2 + n].astype(BF16)


def remote(q, g, inner, outer, far_k, far_v, known, width, depth, scale):
    rows, cols = q.shape
    pairs = cols // width
    hp = width // depth
    far = far_k.shape[0]
    half = far // 2
    return call(
        functools.partial(remote_body, depth, scale, width),
        flops=10 * (far * rows + 2 * BLOCK * BLOCK) * cols,
        moved=rows * cols * 8,
        grid=(pairs,),
        in_specs=[WHOLE] * 7,
        out_specs=[WHOLE] * 6,
        scratch_shapes=[
            pltpu.VMEM((width, far), BF16),
            pltpu.VMEM((2, width, BLOCK), BF16),
            pltpu.VMEM((4, BLOCK, width), F32),
            pltpu.VMEM((hp, rows, width), BF16),
            pltpu.VMEM((hp, rows, width), BF16),
            pltpu.VMEM((2 * hp, BLOCK, BLOCK), F32),
            pltpu.VMEM((2 * hp, BLOCK, BLOCK), F32),
        ],
        out_shape=[
            struct((2, half, cols), F32),
            struct((2, half, cols), BF16),
            struct((2, BLOCK, cols), BF16),
            struct((2, BLOCK, cols), BF16),
            struct((cols, rows), F32),
            struct((pairs, 2, hp, rows), F32),
        ],
    )(q, g, inner, outer, far_k, far_v, known)


def local_body(depth, scale, width, pair, chained, *refs):
    lanes = slice(pair * width, (pair + 1) * width)
    q, k, v, g = (ref.at[:, lanes] for ref in refs[:4])
    part = refs[4].at[lanes]
    final = refs[5].at[pair]
    dq, dk, dv, k_t, dq_t = refs[6 + chained :]
    rows = q.shape[0]
    blocks = rows // BLOCK
    k_t[...] = (k[...].astype(F32) * scale).astype(BF16).T
    for h, mask in enumerate(head_masks(width, depth)):
        hr = slice(h * depth, (h + 1) * depth)
        for b in range(blocks):
            r = slice(b * BLOCK, (b + 1) * BLOCK)
            qs = keep_head(q[r], mask, scale)
            gs = keep_head(g[r], mask)
            reach = near(b, blocks)
            c = slice(reach[0] * BLOCK, (reach[-1] + 1) * BLOCK)
            p = jnp.exp(dot(k[c], qs, NT) - final[0, h : h + 1, r])
            ds = (p * (dot(v[c], gs, NT) - final[1, h : h + 1, r])).astype(BF16)
            v_part = dot(p.astype(BF16), gs, NN)
            k_part = dot(ds, qs, NN)
            for n, j in enumerate(reach):
                rj = slice(j * BLOCK, (j + 1) * BLOCK)
                here = slice(n * BLOCK, (n + 1) * BLOCK)
                if h == 0 and b == near(j, blocks)[0]:
                    dv[rj] = v_part[here]
                    dk[rj] = k_part[here]
                else:
                    dv[rj] += v_part[here]
                    dk[rj] += k_part[here]
            dq_t[hr, r] = part[hr, r] + dot(k_t[hr, c], ds, NN)
    dq[...] = dq_t[...].T.astype(BF16)


def local(q, k, v, g, part, final, before, width, depth, scale, pair):
    rows, cols = q.shape
    extra = [] if before is None else [before]
    return call(
        functools.partial(local_body, depth, scale, width, pair, len(extra)),
        flops=10 * 3 * BLOCK * rows * width,
        moved=rows * width * 24,
        grid=(1,),
        in_specs=[WHOLE] * 6 + [ANY] * len(extra),
        out_specs=[pl.BlockSpec((rows, width), lambda i: (0, pair)), WHOLE, WHOLE],
        out_shape=[struct((rows, cols), BF16)] + [struct((rows, width), F32)] * 2,
        scratch_shapes=[pltpu.VMEM((width, rows), BF16), pltpu.VMEM((width, rows), F32)],
        input_output_aliases={6: 0} if extra else {},
    )(q, k, v, g, part, final, *extra)


def gathered(kept, got, n):
    rows = kept.shape[1]
    total = kept[n]
    for part in got:
        at = rows - part.shape[1]
        more = part[n].astype(F32)
        if at:
            more = jnp.concatenate([jnp.zeros((at, more.shape[1]), F32), more], axis=0)
        total = total + more
    return total


def fold(kept, got, cuts, tokens=(), passed=()):
    cols = kept.shape[-1]
    vmem = pl.BlockSpec(memory_space=pltpu.VMEM)
    extra = list(passed) + list(tokens)
    count = len(got)
    sizes = [b - a for a, b in zip(cuts, cuts[1:])]

    def body(kept, *rest):
        arrived = rest[:count]
        outs = rest[count + len(extra) :]
        for n in range(2):
            total = gathered(kept, arrived, n)
            outs[0][n] = total[: cuts[0]]
            for a, b, out in zip(cuts, cuts[1:], outs[1:]):
                out[n] = total[a:b].astype(BF16)

    return call(
        body,
        moved=kept.size * 8,
        in_specs=[vmem] * (1 + count) + [ANY] * len(extra),
        out_specs=[vmem] * len(cuts) + [ANY] * len(passed),
        out_shape=[struct((2, cuts[0], cols), F32)]
        + [struct((2, size, cols), BF16) for size in sizes]
        + [struct(x.shape, x.dtype) for x in passed],
        input_output_aliases={1 + count + n: len(cuts) + n for n in range(len(passed))},
    )(kept, *got, *extra)


def finish_body(pairs, depth, *refs):
    dk, dv = refs[:pairs], refs[pairs : 2 * pairs]
    from_inner, from_outer, group_pool, whole_pool, kept = refs[2 * pairs : 2 * pairs + 5]
    got = refs[2 * pairs + 5 : -4]
    out_k, out_v, left, total = refs[-4:]
    block = pl.program_id(0)
    rows, cols = kept.shape[1:]
    heads = group_pool.shape[0]
    width = dk[0].shape[1]
    per = BLOCK // SEG1
    count1 = rows * SEG2 // (SEG1 + SEG2)
    blocks = count1 // per

    @pl.when(block == 0)
    def _():
        a, b, c = (t.astype(F32) for t in split(pooling(group_pool[...], whole_pool[...])))
        left[...] = jnp.concatenate([a, a, a, b, b, c], axis=0).T.astype(BF16)
        for n in range(2):
            total[n] = gathered(kept, got, n)

    def emit(halos):
        pick = head_columns(heads, cols, depth)
        for n, (src, dst) in enumerate(((dk, out_k), (dv, out_v))):
            places = [block * per + s for s in range(per)] + [count1 + block]
            found = [jnp.where(pick, total[n, pl.ds(at, 1)], 0.0) for at in places]
            a, b, c = split(jnp.concatenate(found, axis=0))
            spread = dot(left[...], jnp.concatenate([a, b, c, a, b, a], axis=0), NN)
            for halo in halos:
                spread = spread + halo[n].astype(F32)
            for p in range(pairs):
                lanes = slice(p * width, (p + 1) * width)
                dst[:, lanes] = (spread[:, lanes] + src[p][...]).astype(BF16)

    if blocks == 1:
        emit((from_inner, from_outer))
        return
    odd = is_odd()
    at_inner = block == (1 - odd) * (blocks - 1)
    at_outer = block == odd * (blocks - 1)
    pl.when(at_inner)(lambda: emit((from_inner,)))
    pl.when(at_outer)(lambda: emit((from_outer,)))
    pl.when(jnp.logical_not(at_inner | at_outer))(lambda: emit(()))


def finish(dk, dv, from_inner, from_outer, kept, got, group_pool, whole_pool):
    rows, width = dk[0].shape
    pairs = len(dk)
    cols = width * pairs
    depth = cols // group_pool.shape[0]
    tile = pl.BlockSpec((BLOCK, cols), lambda i: (i, 0))
    narrow = pl.BlockSpec((BLOCK, width), lambda i: (i, 0))
    full = lambda x: pl.BlockSpec(x.shape, lambda i: (0,) * x.ndim)
    fixed = [from_inner, from_outer, group_pool, whole_pool, kept] + list(got)
    return call(
        functools.partial(finish_body, pairs, depth),
        moved=rows * cols * 12,
        grid=(rows // BLOCK,),
        in_specs=[narrow] * (2 * pairs) + [full(x) for x in fixed],
        out_specs=[tile, tile],
        out_shape=[struct((rows, cols), BF16)] * 2,
        scratch_shapes=[
            pltpu.VMEM((SEG2, 6 * (BLOCK // SEG1 + 1) * group_pool.shape[0]), BF16),
            pltpu.VMEM(kept.shape, F32),
        ],
    )(*dk, *dv, *fixed)


def shards(query, key, value, out_grad, pool_group, pool_global):
    rows, cols = query.shape
    heads = pool_group.shape[0]
    depth = cols // heads
    scale = 1.0 / math.sqrt(depth)
    width = 128 if cols % 128 == 0 and 128 % depth == 0 else cols
    pairs = cols // width
    devices = lax.axis_size("seq")
    count1 = rows // SEG1
    group_bits = list(range(1, GROUP.bit_length() - 1))
    other_bits = list(range(GROUP.bit_length() - 1, devices.bit_length() - 1))

    def swap(array, *bits):
        mask = sum(1 << bit for bit in bits)
        return lax.ppermute(array, "seq", [(i, i ^ mask) for i in range(devices)])

    def cross(array):
        route = [(i, i + 1) for i in range(1, devices - 1, 2)]
        return lax.ppermute(array, "seq", route + [(b, a) for a, b in route])

    groups, wholes, inner, outer, key, value = pool(key, value, pool_group, pool_global)
    partial = [
        stats(query, key, value, out_grad, width, depth, scale, p) for p in range(pairs)
    ]
    waiting = list(partial)

    def token():
        return [waiting.pop(0)] if waiting else []

    for bit in other_bits[:-1]:
        got = swap(wholes, bit)
        wholes = join([[wholes, got]])[0][0]
    base, far_bit = group_bits[0], other_bits[-1:]
    (pair,) = join([[groups, wholes]])
    here, there = [groups, wholes], []
    there = [swap(pair[0], base)]
    for bit in far_bit:
        here.append(swap(wholes, bit))
        there.append(swap(wholes, base, bit))
    comb, inner = join([here, there], token(), [inner])
    for bit in group_bits[1:]:
        got = swap(comb, bit)
        (comb,) = join([comb, got], token() + token())
    theirs = swap(comb, 0)
    outer = cross(outer)
    inner = swap(inner, 0)

    far_k, far_v, known = far_stats(
        query, out_grad, comb, theirs, partial, width, depth, scale
    )
    kept, sent, inner_d, outer_d, dq_t, final = remote(
        query, out_grad, inner, outer, far_k, far_v, known, width, depth, scale
    )
    got = [swap(sent, 0)]

    query_grad, dk, dv = None, [], []

    def step():
        nonlocal query_grad
        if len(dk) == pairs:
            return []
        query_grad, a, b = local(
            query, key, value, out_grad, dq_t, final, query_grad, width, depth, scale, len(dk)
        )
        dk.append(a)
        dv.append(b)
        return [a]

    from_inner = from_outer = None
    for bit in reversed(group_bits[1:]):
        size = kept.shape[1]
        if from_outer is None:
            kept, sent, inner_d, outer_d = fold(
                kept, got, [size // 2, size], step(), [inner_d, outer_d]
            )
            got = [swap(sent, bit)]
            from_outer = cross(outer_d)
            from_inner = swap(inner_d, 0)
        else:
            kept, sent = fold(kept, got, [size // 2, size], step())
            got = [swap(sent, bit)]
    slot = kept.shape[1] // 2
    own = slot - (slot - count1) // 2 if far_bit else slot
    last = []
    while len(dk) < pairs - 1:
        last = step()
    if far_bit:
        kept, far_here, to_base, far_there = fold(kept, got, [own, slot, slot + own, 2 * slot], last)
        got = [swap(to_base, base), swap(far_here, far_bit[0]), swap(far_there, base, far_bit[0])]
    else:
        kept, to_base = fold(kept, got, [slot, 2 * slot], last)
        got = [swap(to_base, base)]
    for bit in reversed(other_bits[:-1]):
        size = kept.shape[1]
        cut = count1 + (size - count1) // 2
        kept, sent = fold(kept, got, [cut, size])
        got = [swap(sent, bit)]
    while len(dk) < pairs:
        step()
    key_grad, value_grad = finish(
        dk, dv, from_inner, from_outer, kept, got, pool_group, pool_global
    )
    return (query_grad, key_grad, value_grad)


def solution(mesh):
    rows = P("seq", "head")
    in_specs = (rows, rows, rows, rows, P("head", None), P("head", None))
    return jax.shard_map(
        shards, mesh=mesh, in_specs=in_specs, out_specs=(rows, rows, rows), check_vma=False
    )
```

```python
import functools
import math

import jax
import jax.numpy as jnp
from jax import lax
from jax.experimental import pallas as pl
from jax.experimental.pallas import tpu as pltpu
from jax.sharding import PartitionSpec as P


BLOCK = 256
SEG1 = 64
SEG2 = 256
GROUP = 8
NEG = -1e30
F32 = jnp.float32
BF16 = jnp.bfloat16
NT = (((1,), (1,)), ((), ()))
NN = (((1,), (0,)), ((), ()))
VMEM_LIMIT = 32 * 2**20
ANY = pl.BlockSpec(memory_space=pl.ANY)
HBM = pl.BlockSpec(memory_space=pltpu.HBM)
WHOLE = pl.BlockSpec(memory_space=pltpu.VMEM)


def dot(a, b, dims):
    return lax.dot_general(a, b, dims, preferred_element_type=F32)


def struct(shape, dtype):
    return jax.ShapeDtypeStruct(shape, dtype)


def call(body, flops=0, moved=0, vmem=VMEM_LIMIT, **kwargs):
    cost = pl.CostEstimate(flops=int(flops), bytes_accessed=int(moved), transcendentals=0)
    params = pltpu.CompilerParams(vmem_limit_bytes=vmem)
    return pl.pallas_call(body, cost_estimate=cost, compiler_params=params, **kwargs)


def head_masks(width, depth):
    lane = lax.broadcasted_iota(jnp.int32, (1, width), 1)
    return [(lane >= h * depth) & (lane < (h + 1) * depth) for h in range(width // depth)]


def keep_head(rows, mask, scale=None):
    rows = jnp.where(mask, rows, 0)
    if scale is not None:
        rows = rows.astype(F32) * scale
    return rows.astype(BF16)


def near(block, blocks):
    return range(max(block - 1, 0), min(block + 2, blocks))


def is_odd():
    return lax.rem(lax.axis_index("seq"), 2)


def split(x):
    terms = []
    for _ in range(3):
        term = x.astype(BF16)
        terms.append(term)
        x = x - term.astype(F32)
    return terms


def pooling(group_w, whole_w):
    heads = group_w.shape[0]
    per = SEG2 // SEG1
    lane = lax.broadcasted_iota(jnp.int32, (heads, SEG2), 1)
    tiled = jnp.concatenate([group_w] * per, axis=1)
    rows = [
        jnp.where((lane >= s * SEG1) & (lane < (s + 1) * SEG1), tiled, 0.0) for s in range(per)
    ]
    return jnp.concatenate(rows + [whole_w], axis=0)


def head_columns(heads, cols, depth):
    head = lax.broadcasted_iota(jnp.int32, (heads, cols), 0)
    col = lax.broadcasted_iota(jnp.int32, (heads, cols), 1)
    return (col >= head * depth) & (col < (head + 1) * depth)


def pool_body(depth, k, v, group_pool, whole_pool, groups, wholes, inner, outer, *rest):
    *bufs, group_w, whole_w, sems = rest
    rows, cols = bufs[0].shape
    heads = group_w.shape[0]
    chunks = rows // SEG2
    copies = [
        pltpu.make_async_copy(group_pool, group_w, sems.at[2 * chunks]),
        pltpu.make_async_copy(whole_pool, whole_w, sems.at[2 * chunks + 1]),
    ]
    for c in range(chunks):
        r = pl.ds(c * SEG2, SEG2)
        for n, src in enumerate((k, v)):
            copies.append(pltpu.make_async_copy(src.at[r], bufs[n].at[r], sems.at[2 * c + n]))
    for copy in copies:
        copy.start()
    copies[0].wait()
    copies[1].wait()
    per = SEG2 // SEG1
    left = jnp.concatenate(split(pooling(group_w[...], whole_w[...])), axis=0)
    size = (per + 1) * heads
    pick = head_columns(heads, cols, depth)
    sums = [([], []), ([], [])]
    for c in range(chunks):
        for n in range(2):
            copies[2 + 2 * c + n].wait()
            full = dot(left, bufs[n][c * SEG2 : (c + 1) * SEG2], NN)
            full = full[:size] + full[size : 2 * size] + full[2 * size :]
            for s in range(per + 1):
                mine = jnp.where(pick, full[s * heads : (s + 1) * heads], 0.0)
                sums[n][s == per].append(jnp.sum(mine, axis=0, keepdims=True))
    odd = is_odd()
    low = pl.multiple_of(odd * (rows - BLOCK), BLOCK)
    high = pl.multiple_of((1 - odd) * (rows - BLOCK), BLOCK)
    for n in range(2):
        groups[n] = jnp.concatenate(sums[n][0], axis=0).astype(BF16)
        wholes[n] = jnp.concatenate(sums[n][1], axis=0).astype(BF16)
        inner[n] = bufs[n][pl.ds(high, BLOCK)]
        outer[n] = bufs[n][pl.ds(low, BLOCK)]


def pool(k, v, group_pool, whole_pool):
    rows, cols = k.shape
    heads = group_pool.shape[0]
    count1, count2 = rows // SEG1, rows // SEG2
    shapes = [(2, count1, cols), (2, count2, cols), (2, BLOCK, cols), (2, BLOCK, cols)]
    shapes += [k.shape, v.shape]
    inputs = [
        pltpu.with_memory_space_constraint(x, pltpu.HBM) for x in (k, v, group_pool, whole_pool)
    ]
    return call(
        functools.partial(pool_body, cols // heads),
        moved=k.size * 6,
        vmem=16 * 2**20,
        in_specs=[pl.BlockSpec(memory_space=pltpu.HBM)] * 4,
        out_specs=[pl.BlockSpec(memory_space=pltpu.VMEM)] * len(shapes),
        out_shape=[struct(shape, BF16) for shape in shapes],
        scratch_shapes=[
            pltpu.VMEM(group_pool.shape, F32),
            pltpu.VMEM(whole_pool.shape, F32),
            pltpu.SemaphoreType.DMA((2 * count2 + 2,)),
        ],
    )(*inputs)


def join(slots, tokens=(), passed=()):
    flat, plan, count, rows = [], [], 0, 0
    for slot in slots:
        if isinstance(slot, list):
            plan.append((count, len(slot)))
            flat += slot
            rows = sum(part.shape[1] for part in slot)
            count += 1
        else:
            plan.append((count, 0))
            flat.append(slot)
            rows = slot.shape[2]
            count += slot.shape[0]
    cols = flat[0].shape[-1]
    extra = list(passed) + list(tokens)

    def body(*refs):
        out = refs[len(flat) + len(extra)]
        at = 0
        for start, parts in plan:
            if not parts:
                out[start : start + refs[at].shape[0]] = refs[at][...]
                at += 1
                continue
            for n in range(2):
                pieces = [refs[at + i][n].astype(F32) for i in range(parts)]
                out[start, n] = jnp.concatenate(pieces, axis=0).astype(BF16)
            at += parts

    vmem = pl.BlockSpec(memory_space=pltpu.VMEM)
    return call(
        body,
        moved=4 * count * 2 * rows * cols,
        in_specs=[vmem] * len(flat) + [ANY] * len(extra),
        out_specs=[vmem] + [ANY] * len(passed),
        out_shape=[struct((count, 2, rows, cols), BF16)]
        + [struct(x.shape, x.dtype) for x in passed],
        input_output_aliases={len(flat) + n: 1 + n for n in range(len(passed))},
    )(*flat, *extra)


def merge(state, s_all, d_all, chunk=64):
    for c in range(0, s_all.shape[0], chunk):
        s = s_all[c : c + chunk]
        count = s.shape[0] // 8
        s = s.reshape(count, 8, s.shape[1])
        d = d_all[c : c + chunk].reshape(s.shape)
        here = jnp.max(s, axis=0)
        top = here if state is None else jnp.maximum(state[0], here)
        e = jnp.exp(s - top[None])
        total = jnp.sum(e, axis=0)
        inner = jnp.sum(e * d, axis=0)
        if state is not None:
            fade = jnp.exp(state[0] - top)
            total = total + state[1] * fade
            inner = inner + state[2] * fade
        state = (top, total, inner)
    return state


def stats_body(depth, scale, width, pair, *refs):
    lanes = slice(pair * width, (pair + 1) * width)
    q, k, v, g = (ref.at[:, lanes] for ref in refs[:4])
    out = refs[4]
    rows = q.shape[0]
    blocks = rows // BLOCK
    for h, mask in enumerate(head_masks(width, depth)):
        for b in range(blocks):
            r = slice(b * BLOCK, (b + 1) * BLOCK)
            qs = keep_head(q[r], mask, scale)
            gs = keep_head(g[r], mask)
            c = slice(near(b, blocks)[0] * BLOCK, (near(b, blocks)[-1] + 1) * BLOCK)
            top, total, inner = merge(None, dot(k[c], qs, NT), dot(v[c], gs, NT))
            most = jnp.max(top, axis=0, keepdims=True)
            fade = jnp.exp(top - most)
            out[0, h : h + 1, r] = most
            out[1, h : h + 1, r] = jnp.sum(total * fade, axis=0, keepdims=True)
            out[2, h : h + 1, r] = jnp.sum(inner * fade, axis=0, keepdims=True)


def stats(q, k, v, g, width, depth, scale, pair):
    rows = q.shape[0]
    hp = width // depth
    return call(
        functools.partial(stats_body, depth, scale, width, pair),
        flops=2 * 2 * 3 * BLOCK * rows * width,
        moved=rows * width * 8,
        in_specs=[WHOLE] * 4,
        out_specs=WHOLE,
        out_shape=struct((3, hp, rows), F32),
    )(q, k, v, g)


def far_body(depth, scale, width, pairs, q, g, mine, theirs, *rest):
    partial = rest[:pairs]
    far_k, far_v, known = rest[pairs:]
    rows = q.shape[0]
    slots, _, per, _ = mine.shape
    half = slots * per
    pair = pl.program_id(0)
    lanes = pl.ds(pl.multiple_of(pair * width, width), width)
    q, g, far_k, far_v = (ref.at[:, lanes] for ref in (q, g, far_k, far_v))
    mine, theirs = (ref.at[:, :, :, lanes] for ref in (mine, theirs))
    out = known.at[pair]
    for n, far in enumerate((far_k, far_v)):
        for m, src in enumerate((mine, theirs)):
            for s in range(slots):
                at = m * half + s * per
                far[at : at + per] = src[s, n]
    for h, mask in enumerate(head_masks(width, depth)):
        for b in range(rows // BLOCK):
            r = slice(b * BLOCK, (b + 1) * BLOCK)
            qs = keep_head(q[r], mask, scale)
            gs = keep_head(g[r], mask)
            old = [partial[0][m, h : h + 1, r] for m in range(3)]
            for n in range(1, pairs):
                old = [
                    jnp.where(pair == n, partial[n][m, h : h + 1, r], old[m]) for m in range(3)
                ]
            state = merge(None, dot(far_k[...], qs, NT), dot(far_v[...], gs, NT))
            for m, value in enumerate(settle(old, state)):
                out[m, h : h + 1, r] = value


def settle(old, state):
    top8, total8, inner8 = state
    top = jnp.maximum(old[0], jnp.max(top8, axis=0, keepdims=True))
    fade = jnp.exp(old[0] - top)
    fade8 = jnp.exp(top8 - top)
    total = old[1] * fade + jnp.sum(total8 * fade8, axis=0, keepdims=True)
    dots = old[2] * fade + jnp.sum(inner8 * fade8, axis=0, keepdims=True)
    return top, total, dots


def far_stats(q, g, mine, theirs, partial, width, depth, scale):
    rows, cols = q.shape
    pairs = cols // width
    hp = width // depth
    slots, _, per, _ = mine.shape
    far = 2 * slots * per
    return call(
        functools.partial(far_body, depth, scale, width, pairs),
        flops=4 * far * rows * cols,
        moved=rows * cols * 4,
        grid=(pairs,),
        in_specs=[WHOLE] * (4 + pairs),
        out_specs=[WHOLE] * 3,
        out_shape=[struct((far, cols), BF16)] * 2 + [struct((pairs, 3, hp, rows), F32)],
    )(q, g, mine, theirs, *partial)


def remote_body(depth, scale, width, q, g, inner, outer, far_k, far_v, known, *rest):
    far_kt, near_t, near_d, qs, gs, s_held, d_held = rest[6:]
    rows = q.shape[0]
    blocks = rows // BLOCK
    half = far_k.shape[0] // 2
    masks = head_masks(width, depth)
    pair = pl.program_id(0)
    lanes = pl.ds(pl.multiple_of(pair * width, width), width)
    q, g, far_k, far_v = (ref.at[:, lanes] for ref in (q, g, far_k, far_v))
    inner, outer = (ref.at[:, :, lanes] for ref in (inner, outer))
    kept, sent, inner_d, outer_d = (ref.at[:, :, lanes] for ref in rest[:4])
    dq_t = rest[4].at[lanes]
    final = rest[5].at[pair]
    known = known.at[pair]
    far_kt[...] = (far_k[...].astype(F32) * scale).astype(BF16).T
    near_t[0] = (inner[0].astype(F32) * scale).astype(BF16).T
    near_t[1] = (outer[0].astype(F32) * scale).astype(BF16).T
    scaled = (q[...].astype(F32) * scale).astype(BF16)
    for h, mask in enumerate(masks):
        qs[h] = jnp.where(mask, scaled, 0).astype(BF16)
        gs[h] = jnp.where(mask, g[...], 0).astype(BF16)
    odd = is_odd()
    position = lax.axis_index("seq")
    ends = (position == 0) | (position == lax.axis_size("seq") - 1)
    missing = jnp.where(ends, NEG, 0.0)
    places = [
        pl.ds(pl.multiple_of(n * ((blocks - 1) * BLOCK), BLOCK), BLOCK) for n in (1 - odd, odd)
    ]
    halos = ((inner, None), (outer, missing))
    final[0] = known[0] + jnp.log(known[1])
    final[1] = known[2] / known[1]
    for h in range(len(masks)):
        old = None
        for n, ((halo, bias), r) in enumerate(zip(halos, places)):
            if old is None or blocks > 1:
                old = [known[m, h : h + 1, r] for m in range(3)]
            s = dot(halo[0], qs[h, r], NT)
            if bias is not None:
                s = s + bias
            d = dot(halo[1], gs[h, r], NT)
            s_held[2 * h + n] = s
            d_held[2 * h + n] = d
            old = settle(old, merge(None, s, d))
            final[0, h : h + 1, r] = old[0] + jnp.log(old[1])
            final[1, h : h + 1, r] = old[2] / old[1]
    totals = [None, None]
    for h in range(len(masks)):
        hr = slice(h * depth, (h + 1) * depth)
        p = jnp.exp(dot(far_k[...], qs[h], NT) - final[0, h : h + 1, :])
        ds = (p * (dot(far_v[...], gs[h], NT) - final[1, h : h + 1, :])).astype(BF16)
        parts = (dot(ds, qs[h], NN), dot(p.astype(BF16), gs[h], NN))
        totals = [new if old is None else old + new for old, new in zip(totals, parts)]
        dq_t[hr] = dot(far_kt[hr], ds, NN)
        for n, r in enumerate(places):
            p = jnp.exp(s_held[2 * h + n] - final[0, h : h + 1, r])
            ds = (p * (d_held[2 * h + n] - final[1, h : h + 1, r])).astype(BF16)
            parts = (dot(ds, qs[h, r], NN), dot(p.astype(BF16), gs[h, r], NN))
            for m, part in enumerate(parts):
                if h == 0:
                    near_d[2 * n + m] = part
                else:
                    near_d[2 * n + m] += part
            dq_t[hr, r] += dot(near_t[n, hr], ds, NN)
    for n in range(2):
        kept[n] = totals[n][:half]
        sent[n] = totals[n][half:].astype(BF16)
        inner_d[n] = near_d[n].astype(BF16)
        outer_d[n] = near_d[2 + n].astype(BF16)


def remote(q, g, inner, outer, far_k, far_v, known, width, depth, scale):
    rows, cols = q.shape
    pairs = cols // width
    hp = width // depth
    far = far_k.shape[0]
    half = far // 2
    return call(
        functools.partial(remote_body, depth, scale, width),
        flops=10 * (far * rows + 2 * BLOCK * BLOCK) * cols,
        moved=rows * cols * 8,
        grid=(pairs,),
        in_specs=[WHOLE] * 7,
        out_specs=[WHOLE] * 6,
        scratch_shapes=[
            pltpu.VMEM((width, far), BF16),
            pltpu.VMEM((2, width, BLOCK), BF16),
            pltpu.VMEM((4, BLOCK, width), F32),
            pltpu.VMEM((hp, rows, width), BF16),
            pltpu.VMEM((hp, rows, width), BF16),
            pltpu.VMEM((2 * hp, BLOCK, BLOCK), F32),
            pltpu.VMEM((2 * hp, BLOCK, BLOCK), F32),
        ],
        out_shape=[
            struct((2, half, cols), F32),
            struct((2, half, cols), BF16),
            struct((2, BLOCK, cols), BF16),
            struct((2, BLOCK, cols), BF16),
            struct((cols, rows), F32),
            struct((pairs, 2, hp, rows), F32),
        ],
    )(q, g, inner, outer, far_k, far_v, known)


def local_body(depth, scale, width, pair, chained, *refs):
    lanes = slice(pair * width, (pair + 1) * width)
    q, k, v, g = (ref.at[:, lanes] for ref in refs[:4])
    part = refs[4].at[lanes]
    final = refs[5].at[pair]
    dq, dk, dv, *rest = refs[6 + chained :]
    k_t, dq_t = rest[chained > 0 :][:2]
    if chained:
        earlier = slice((pair - 1) * width, pair * width)
        copy = pltpu.make_async_copy(refs[6], rest[0].at[:, earlier], rest[3])
        copy.start()
    rows = q.shape[0]
    blocks = rows // BLOCK
    k_t[...] = (k[...].astype(F32) * scale).astype(BF16).T
    for h, mask in enumerate(head_masks(width, depth)):
        hr = slice(h * depth, (h + 1) * depth)
        for b in range(blocks):
            r = slice(b * BLOCK, (b + 1) * BLOCK)
            qs = keep_head(q[r], mask, scale)
            gs = keep_head(g[r], mask)
            reach = near(b, blocks)
            c = slice(reach[0] * BLOCK, (reach[-1] + 1) * BLOCK)
            p = jnp.exp(dot(k[c], qs, NT) - final[0, h : h + 1, r])
            ds = (p * (dot(v[c], gs, NT) - final[1, h : h + 1, r])).astype(BF16)
            v_part = dot(p.astype(BF16), gs, NN)
            k_part = dot(ds, qs, NN)
            for n, j in enumerate(reach):
                rj = slice(j * BLOCK, (j + 1) * BLOCK)
                here = slice(n * BLOCK, (n + 1) * BLOCK)
                if h == 0 and b == near(j, blocks)[0]:
                    dv[rj] = v_part[here]
                    dk[rj] = k_part[here]
                else:
                    dv[rj] += v_part[here]
                    dk[rj] += k_part[here]
            dq_t[hr, r] = part[hr, r] + dot(k_t[hr, c], ds, NN)
    dq[...] = dq_t[...].T.astype(BF16)
    if chained:
        copy.wait()


def local(q, k, v, g, part, final, earlier, width, depth, scale, pair):
    rows, cols = q.shape
    chained = len(earlier)
    tile, wide = struct((rows, width), BF16), struct((rows, width), F32)
    return call(
        functools.partial(local_body, depth, scale, width, pair, chained),
        flops=10 * 3 * BLOCK * rows * width,
        moved=rows * width * 24,
        in_specs=[WHOLE] * 6 + [WHOLE, ANY][:chained],
        out_specs=[WHOLE] * 3 + [HBM] * (chained > 0),
        out_shape=[tile, wide, wide] + [struct((rows, cols), BF16)] * (chained > 0),
        scratch_shapes=[pltpu.VMEM((width, rows), BF16), pltpu.VMEM((width, rows), F32)]
        + [pltpu.SemaphoreType.DMA] * (chained > 0),
        input_output_aliases={7: 3} if chained == 2 else {},
    )(q, k, v, g, part, final, *earlier)


def gathered(kept, got, n):
    rows = kept.shape[1]
    total = kept[n]
    for part in got:
        at = rows - part.shape[1]
        more = part[n].astype(F32)
        if at:
            more = jnp.concatenate([jnp.zeros((at, more.shape[1]), F32), more], axis=0)
        total = total + more
    return total


def fold(kept, got, cuts, tokens=(), passed=()):
    cols = kept.shape[-1]
    vmem = pl.BlockSpec(memory_space=pltpu.VMEM)
    extra = list(passed) + list(tokens)
    count = len(got)
    sizes = [b - a for a, b in zip(cuts, cuts[1:])]

    def body(kept, *rest):
        arrived = rest[:count]
        outs = rest[count + len(extra) :]
        for n in range(2):
            total = gathered(kept, arrived, n)
            outs[0][n] = total[: cuts[0]]
            for a, b, out in zip(cuts, cuts[1:], outs[1:]):
                out[n] = total[a:b].astype(BF16)

    return call(
        body,
        moved=kept.size * 8,
        in_specs=[vmem] * (1 + count) + [ANY] * len(extra),
        out_specs=[vmem] * len(cuts) + [ANY] * len(passed),
        out_shape=[struct((2, cuts[0], cols), F32)]
        + [struct((2, size, cols), BF16) for size in sizes]
        + [struct(x.shape, x.dtype) for x in passed],
        input_output_aliases={1 + count + n: len(cuts) + n for n in range(len(passed))},
    )(kept, *got, *extra)


def finish_body(pairs, depth, count, *refs):
    dk, dv = refs[:pairs], refs[pairs : 2 * pairs]
    from_inner, from_outer, group_pool, whole_pool, kept = refs[2 * pairs : 2 * pairs + 5]
    got = refs[2 * pairs + 5 : 2 * pairs + 5 + count]
    tile = refs[2 * pairs + 5 + count]
    out_k, out_v, out_q, left, total, sem = refs[-6:]
    block = pl.program_id(0)
    last = slice((pairs - 1) * tile.shape[1], pairs * tile.shape[1])
    copy = pltpu.make_async_copy(tile, out_q.at[:, last], sem)
    pl.when(block == 0)(copy.start)
    rows, cols = kept.shape[1:]
    heads = group_pool.shape[0]
    width = dk[0].shape[1]
    per = BLOCK // SEG1
    count1 = rows * SEG2 // (SEG1 + SEG2)
    blocks = count1 // per

    @pl.when(block == 0)
    def _():
        a, b, c = (t.astype(F32) for t in split(pooling(group_pool[...], whole_pool[...])))
        left[...] = jnp.concatenate([a, a, a, b, b, c], axis=0).T.astype(BF16)
        for n in range(2):
            total[n] = gathered(kept, got, n)

    def emit(halos):
        pick = head_columns(heads, cols, depth)
        for n, (src, dst) in enumerate(((dk, out_k), (dv, out_v))):
            places = [block * per + s for s in range(per)] + [count1 + block]
            found = [jnp.where(pick, total[n, pl.ds(at, 1)], 0.0) for at in places]
            a, b, c = split(jnp.concatenate(found, axis=0))
            spread = dot(left[...], jnp.concatenate([a, b, c, a, b, a], axis=0), NN)
            for halo in halos:
                spread = spread + halo[n].astype(F32)
            for p in range(pairs):
                lanes = slice(p * width, (p + 1) * width)
                dst[:, lanes] = (spread[:, lanes] + src[p][...]).astype(BF16)

    if blocks == 1:
        emit((from_inner, from_outer))
        copy.wait()
        return
    odd = is_odd()
    at_inner = block == (1 - odd) * (blocks - 1)
    at_outer = block == odd * (blocks - 1)
    pl.when(at_inner)(lambda: emit((from_inner,)))
    pl.when(at_outer)(lambda: emit((from_outer,)))
    pl.when(jnp.logical_not(at_inner | at_outer))(lambda: emit(()))
    pl.when(block == blocks - 1)(copy.wait)


def finish(dk, dv, from_inner, from_outer, kept, got, group_pool, whole_pool, earlier):
    rows, width = dk[0].shape
    pairs = len(dk)
    cols = width * pairs
    depth = cols // group_pool.shape[0]
    out = pl.BlockSpec((BLOCK, cols), lambda i: (i, 0))
    narrow = pl.BlockSpec((BLOCK, width), lambda i: (i, 0))
    fixed = [from_inner, from_outer, group_pool, whole_pool, kept] + list(got)
    place = 2 * pairs + len(fixed) + 1
    return call(
        functools.partial(finish_body, pairs, depth, len(got)),
        moved=rows * cols * 12,
        grid=(rows // BLOCK,),
        in_specs=[narrow] * (2 * pairs)
        + [WHOLE] * (len(fixed) + 1)
        + [ANY] * (len(earlier) - 1),
        out_specs=[out, out, HBM],
        out_shape=[struct((rows, cols), BF16)] * 3,
        scratch_shapes=[
            pltpu.VMEM((SEG2, 6 * (BLOCK // SEG1 + 1) * group_pool.shape[0]), BF16),
            pltpu.VMEM(kept.shape, F32),
            pltpu.SemaphoreType.DMA,
        ],
        input_output_aliases={place: 2} if len(earlier) == 2 else {},
    )(*dk, *dv, *fixed, *earlier)


def shards(query, key, value, out_grad, pool_group, pool_global):
    rows, cols = query.shape
    heads = pool_group.shape[0]
    depth = cols // heads
    scale = 1.0 / math.sqrt(depth)
    width = 128 if cols % 128 == 0 and 128 % depth == 0 else cols
    pairs = cols // width
    devices = lax.axis_size("seq")
    count1 = rows // SEG1
    group_bits = list(range(1, GROUP.bit_length() - 1))
    other_bits = list(range(GROUP.bit_length() - 1, devices.bit_length() - 1))

    def swap(array, *bits):
        mask = sum(1 << bit for bit in bits)
        return lax.ppermute(array, "seq", [(i, i ^ mask) for i in range(devices)])

    def cross(array):
        route = [(i, i + 1) for i in range(1, devices - 1, 2)]
        return lax.ppermute(array, "seq", route + [(b, a) for a, b in route])

    groups, wholes, inner, outer, key, value = pool(key, value, pool_group, pool_global)
    partial = [
        stats(query, key, value, out_grad, width, depth, scale, p) for p in range(pairs)
    ]
    waiting = list(partial)

    def token():
        return [waiting.pop(0)] if waiting else []

    for bit in other_bits[:-1]:
        got = swap(wholes, bit)
        wholes = join([[wholes, got]])[0][0]
    base, far_bit = group_bits[0], other_bits[-1:]
    (pair,) = join([[groups, wholes]])
    here, there = [groups, wholes], []
    there = [swap(pair[0], base)]
    for bit in far_bit:
        here.append(swap(wholes, bit))
        there.append(swap(wholes, base, bit))
    comb, inner = join([here, there], token(), [inner])
    for bit in group_bits[1:]:
        got = swap(comb, bit)
        (comb,) = join([comb, got], token() + token())
    theirs = swap(comb, 0)
    outer = cross(outer)
    inner = swap(inner, 0)

    far_k, far_v, known = far_stats(
        query, out_grad, comb, theirs, partial, width, depth, scale
    )
    kept, sent, inner_d, outer_d, dq_t, final = remote(
        query, out_grad, inner, outer, far_k, far_v, known, width, depth, scale
    )
    got = [swap(sent, 0)]

    earlier, dk, dv = [], [], []

    def step():
        nonlocal earlier
        if len(dk) == pairs:
            return []
        tile, a, b, *rest = local(
            query, key, value, out_grad, dq_t, final, earlier, width, depth, scale, len(dk)
        )
        earlier = [tile] + rest
        dk.append(a)
        dv.append(b)
        return [a]

    from_inner = from_outer = None
    for bit in reversed(group_bits[1:]):
        size = kept.shape[1]
        if from_outer is None:
            kept, sent, inner_d, outer_d = fold(
                kept, got, [size // 2, size], step(), [inner_d, outer_d]
            )
            got = [swap(sent, bit)]
            from_outer = cross(outer_d)
            from_inner = swap(inner_d, 0)
        else:
            kept, sent = fold(kept, got, [size // 2, size], step())
            got = [swap(sent, bit)]
    slot = kept.shape[1] // 2
    own = slot - (slot - count1) // 2 if far_bit else slot
    last = []
    while len(dk) < pairs - 1:
        last = step()
    if far_bit:
        kept, far_here, to_base, far_there = fold(kept, got, [own, slot, slot + own, 2 * slot], last)
        got = [swap(to_base, base), swap(far_here, far_bit[0]), swap(far_there, base, far_bit[0])]
    else:
        kept, to_base = fold(kept, got, [slot, 2 * slot], last)
        got = [swap(to_base, base)]
    for bit in reversed(other_bits[:-1]):
        size = kept.shape[1]
        cut = count1 + (size - count1) // 2
        kept, sent = fold(kept, got, [cut, size])
        got = [swap(sent, bit)]
    while len(dk) < pairs:
        step()
    key_grad, value_grad, query_grad = finish(
        dk, dv, from_inner, from_outer, kept, got, pool_group, pool_global, earlier
    )
    return (query_grad, key_grad, value_grad)


def solution(mesh):
    rows = P("seq", "head")
    in_specs = (rows, rows, rows, rows, P("head", None), P("head", None))
    return jax.shard_map(
        shards, mesh=mesh, in_specs=in_specs, out_specs=(rows, rows, rows), check_vma=False
    )
```

```python
import functools
import math

import jax
import jax.numpy as jnp
from jax import lax
from jax.experimental import pallas as pl
from jax.experimental.pallas import tpu as pltpu
from jax.sharding import PartitionSpec as P


BLOCK = 256
SEG1 = 64
SEG2 = 256
GROUP = 8
NEG = -1e30
F32 = jnp.float32
BF16 = jnp.bfloat16
NT = (((1,), (1,)), ((), ()))
NN = (((1,), (0,)), ((), ()))
VMEM_LIMIT = 32 * 2**20
ANY = pl.BlockSpec(memory_space=pl.ANY)
HBM = pl.BlockSpec(memory_space=pltpu.HBM)
WHOLE = pl.BlockSpec(memory_space=pltpu.VMEM)


def dot(a, b, dims):
    return lax.dot_general(a, b, dims, preferred_element_type=F32)


def struct(shape, dtype):
    return jax.ShapeDtypeStruct(shape, dtype)


def call(body, flops=0, moved=0, vmem=VMEM_LIMIT, **kwargs):
    cost = pl.CostEstimate(flops=int(flops), bytes_accessed=int(moved), transcendentals=0)
    params = pltpu.CompilerParams(vmem_limit_bytes=vmem)
    return pl.pallas_call(body, cost_estimate=cost, compiler_params=params, **kwargs)


def head_masks(width, depth):
    lane = lax.broadcasted_iota(jnp.int32, (1, width), 1)
    return [(lane >= h * depth) & (lane < (h + 1) * depth) for h in range(width // depth)]


def keep_head(rows, mask, scale=None):
    rows = jnp.where(mask, rows, 0)
    if scale is not None:
        rows = rows.astype(F32) * scale
    return rows.astype(BF16)


def near(block, blocks):
    return range(max(block - 1, 0), min(block + 2, blocks))


def is_odd():
    return lax.rem(lax.axis_index("seq"), 2)


def split(x):
    terms = []
    for _ in range(3):
        term = x.astype(BF16)
        terms.append(term)
        x = x - term.astype(F32)
    return terms


def pooling(group_w, whole_w):
    heads = group_w.shape[0]
    per = SEG2 // SEG1
    lane = lax.broadcasted_iota(jnp.int32, (heads, SEG2), 1)
    tiled = jnp.concatenate([group_w] * per, axis=1)
    rows = [
        jnp.where((lane >= s * SEG1) & (lane < (s + 1) * SEG1), tiled, 0.0) for s in range(per)
    ]
    return jnp.concatenate(rows + [whole_w], axis=0)


def head_columns(heads, cols, depth):
    head = lax.broadcasted_iota(jnp.int32, (heads, cols), 0)
    col = lax.broadcasted_iota(jnp.int32, (heads, cols), 1)
    return (col >= head * depth) & (col < (head + 1) * depth)


def pool_body(depth, k, v, group_pool, whole_pool, groups, wholes, inner, outer, *rest):
    *bufs, group_w, whole_w, sems = rest
    rows, cols = bufs[0].shape
    heads = group_w.shape[0]
    chunks = rows // SEG2
    copies = [
        pltpu.make_async_copy(group_pool, group_w, sems.at[2 * chunks]),
        pltpu.make_async_copy(whole_pool, whole_w, sems.at[2 * chunks + 1]),
    ]
    for c in range(chunks):
        r = pl.ds(c * SEG2, SEG2)
        for n, src in enumerate((k, v)):
            copies.append(pltpu.make_async_copy(src.at[r], bufs[n].at[r], sems.at[2 * c + n]))
    for copy in copies:
        copy.start()
    copies[0].wait()
    copies[1].wait()
    per = SEG2 // SEG1
    left = jnp.concatenate(split(pooling(group_w[...], whole_w[...])), axis=0)
    size = (per + 1) * heads
    pick = head_columns(heads, cols, depth)
    sums = [([], []), ([], [])]
    for c in range(chunks):
        for n in range(2):
            copies[2 + 2 * c + n].wait()
            full = dot(left, bufs[n][c * SEG2 : (c + 1) * SEG2], NN)
            full = full[:size] + full[size : 2 * size] + full[2 * size :]
            for s in range(per + 1):
                mine = jnp.where(pick, full[s * heads : (s + 1) * heads], 0.0)
                sums[n][s == per].append(jnp.sum(mine, axis=0, keepdims=True))
    odd = is_odd()
    low = pl.multiple_of(odd * (rows - BLOCK), BLOCK)
    high = pl.multiple_of((1 - odd) * (rows - BLOCK), BLOCK)
    for n in range(2):
        groups[n] = jnp.concatenate(sums[n][0], axis=0).astype(BF16)
        wholes[n] = jnp.concatenate(sums[n][1], axis=0).astype(BF16)
        inner[n] = bufs[n][pl.ds(high, BLOCK)]
        outer[n] = bufs[n][pl.ds(low, BLOCK)]


def pool(k, v, group_pool, whole_pool):
    rows, cols = k.shape
    heads = group_pool.shape[0]
    count1, count2 = rows // SEG1, rows // SEG2
    shapes = [(2, count1, cols), (2, count2, cols), (2, BLOCK, cols), (2, BLOCK, cols)]
    shapes += [k.shape, v.shape]
    inputs = [
        pltpu.with_memory_space_constraint(x, pltpu.HBM) for x in (k, v, group_pool, whole_pool)
    ]
    return call(
        functools.partial(pool_body, cols // heads),
        moved=k.size * 6,
        vmem=16 * 2**20,
        in_specs=[pl.BlockSpec(memory_space=pltpu.HBM)] * 4,
        out_specs=[pl.BlockSpec(memory_space=pltpu.VMEM)] * len(shapes),
        out_shape=[struct(shape, BF16) for shape in shapes],
        scratch_shapes=[
            pltpu.VMEM(group_pool.shape, F32),
            pltpu.VMEM(whole_pool.shape, F32),
            pltpu.SemaphoreType.DMA((2 * count2 + 2,)),
        ],
    )(*inputs)


def join(slots, tokens=(), passed=()):
    flat, plan, count, rows = [], [], 0, 0
    for slot in slots:
        if isinstance(slot, list):
            plan.append((count, len(slot)))
            flat += slot
            rows = sum(part.shape[1] for part in slot)
            count += 1
        else:
            plan.append((count, 0))
            flat.append(slot)
            rows = slot.shape[2]
            count += slot.shape[0]
    cols = flat[0].shape[-1]
    extra = list(passed) + list(tokens)

    def body(*refs):
        out = refs[len(flat) + len(extra)]
        at = 0
        for start, parts in plan:
            if not parts:
                out[start : start + refs[at].shape[0]] = refs[at][...]
                at += 1
                continue
            for n in range(2):
                pieces = [refs[at + i][n].astype(F32) for i in range(parts)]
                out[start, n] = jnp.concatenate(pieces, axis=0).astype(BF16)
            at += parts

    vmem = pl.BlockSpec(memory_space=pltpu.VMEM)
    return call(
        body,
        moved=4 * count * 2 * rows * cols,
        in_specs=[vmem] * len(flat) + [ANY] * len(extra),
        out_specs=[vmem] + [ANY] * len(passed),
        out_shape=[struct((count, 2, rows, cols), BF16)]
        + [struct(x.shape, x.dtype) for x in passed],
        input_output_aliases={len(flat) + n: 1 + n for n in range(len(passed))},
    )(*flat, *extra)


def merge(state, s_all, d_all, chunk=64):
    for c in range(0, s_all.shape[0], chunk):
        s = s_all[c : c + chunk]
        count = s.shape[0] // 8
        s = s.reshape(count, 8, s.shape[1])
        d = d_all[c : c + chunk].reshape(s.shape)
        here = jnp.max(s, axis=0)
        top = here if state is None else jnp.maximum(state[0], here)
        e = jnp.exp(s - top[None])
        total = jnp.sum(e, axis=0)
        inner = jnp.sum(e * d, axis=0)
        if state is not None:
            fade = jnp.exp(state[0] - top)
            total = total + state[1] * fade
            inner = inner + state[2] * fade
        state = (top, total, inner)
    return state


def stats_body(depth, scale, width, pair, *refs):
    lanes = slice(pair * width, (pair + 1) * width)
    q, k, v, g = (ref.at[:, lanes] for ref in refs[:4])
    out = refs[4]
    rows = q.shape[0]
    blocks = rows // BLOCK
    for h, mask in enumerate(head_masks(width, depth)):
        for b in range(blocks):
            r = slice(b * BLOCK, (b + 1) * BLOCK)
            qs = keep_head(q[r], mask, scale)
            gs = keep_head(g[r], mask)
            c = slice(near(b, blocks)[0] * BLOCK, (near(b, blocks)[-1] + 1) * BLOCK)
            top, total, inner = merge(None, dot(k[c], qs, NT), dot(v[c], gs, NT))
            most = jnp.max(top, axis=0, keepdims=True)
            fade = jnp.exp(top - most)
            out[0, h : h + 1, r] = most
            out[1, h : h + 1, r] = jnp.sum(total * fade, axis=0, keepdims=True)
            out[2, h : h + 1, r] = jnp.sum(inner * fade, axis=0, keepdims=True)


def stats(q, k, v, g, width, depth, scale, pair):
    rows = q.shape[0]
    hp = width // depth
    return call(
        functools.partial(stats_body, depth, scale, width, pair),
        flops=2 * 2 * 3 * BLOCK * rows * width,
        moved=rows * width * 8,
        in_specs=[WHOLE] * 4,
        out_specs=WHOLE,
        out_shape=struct((3, hp, rows), F32),
    )(q, k, v, g)


def place_slots(sources, far, n):
    at = 0
    for src in sources:
        for s in range(src.shape[0]):
            far[at : at + src.shape[2]] = src[s, n]
            at += src.shape[2]


def far_body(depth, scale, width, pairs, q, g, mine, *rest):
    partial = rest[:pairs]
    qs, gs, known, near_k, near_v = rest[pairs:]
    rows = q.shape[0]
    pair = pl.program_id(0)
    lanes = pl.ds(pl.multiple_of(pair * width, width), width)
    q, g = (ref.at[:, lanes] for ref in (q, g))
    qs, gs = (ref.at[:, :, lanes] for ref in (qs, gs))
    mine = mine.at[:, :, :, lanes]
    out = known.at[pair]
    place_slots((mine,), near_k, 0)
    place_slots((mine,), near_v, 1)
    for h, mask in enumerate(head_masks(width, depth)):
        for b in range(rows // BLOCK):
            r = slice(b * BLOCK, (b + 1) * BLOCK)
            q_rows = keep_head(q[r], mask, scale)
            g_rows = keep_head(g[r], mask)
            qs[h, r] = q_rows
            gs[h, r] = g_rows
            old = [partial[0][m, h : h + 1, r] for m in range(3)]
            for n in range(1, pairs):
                old = [
                    jnp.where(pair == n, partial[n][m, h : h + 1, r], old[m]) for m in range(3)
                ]
            state = merge(None, dot(near_k[...], q_rows, NT), dot(near_v[...], g_rows, NT))
            for m, value in enumerate(settle(old, state)):
                out[m, h : h + 1, r] = value


def more_body(width, qs, gs, mine, theirs, known, far_k, far_v, out):
    rows = qs.shape[1]
    pair = pl.program_id(0)
    lanes = pl.ds(pl.multiple_of(pair * width, width), width)
    qs, gs = (ref.at[:, :, lanes] for ref in (qs, gs))
    mine, theirs = (ref.at[:, :, :, lanes] for ref in (mine, theirs))
    far_k, far_v = (ref.at[:, lanes] for ref in (far_k, far_v))
    known, out = known.at[pair], out.at[pair]
    place_slots((mine, theirs), far_k, 0)
    place_slots((mine, theirs), far_v, 1)
    half = far_k.shape[0] // 2
    for h in range(qs.shape[0]):
        for b in range(rows // BLOCK):
            r = slice(b * BLOCK, (b + 1) * BLOCK)
            old = [known[m, h : h + 1, r] for m in range(3)]
            s = dot(far_k[half:], qs[h, r], NT)
            d = dot(far_v[half:], gs[h, r], NT)
            for m, value in enumerate(settle(old, merge(None, s, d))):
                out[m, h : h + 1, r] = value


def settle(old, state):
    top8, total8, inner8 = state
    top = jnp.maximum(old[0], jnp.max(top8, axis=0, keepdims=True))
    fade = jnp.exp(old[0] - top)
    fade8 = jnp.exp(top8 - top)
    total = old[1] * fade + jnp.sum(total8 * fade8, axis=0, keepdims=True)
    dots = old[2] * fade + jnp.sum(inner8 * fade8, axis=0, keepdims=True)
    return top, total, dots


def far_stats(q, g, mine, partial, width, depth, scale):
    rows, cols = q.shape
    pairs = cols // width
    hp = width // depth
    half = mine.shape[0] * mine.shape[2]
    return call(
        functools.partial(far_body, depth, scale, width, pairs),
        flops=4 * half * rows * cols,
        moved=rows * cols * 4,
        grid=(pairs,),
        in_specs=[WHOLE] * (3 + pairs),
        out_specs=[WHOLE] * 3,
        out_shape=[struct((hp, rows, cols), BF16)] * 2 + [struct((pairs, 3, hp, rows), F32)],
        scratch_shapes=[pltpu.VMEM((half, width), BF16)] * 2,
    )(q, g, mine, *partial)


def more_stats(qs, gs, mine, theirs, known, width):
    rows, cols = qs.shape[1:]
    far = 2 * mine.shape[0] * mine.shape[2]
    return call(
        functools.partial(more_body, width),
        flops=2 * far * rows * cols,
        moved=rows * cols * 4,
        grid=(cols // width,),
        in_specs=[WHOLE] * 5,
        out_specs=[WHOLE] * 3,
        out_shape=[struct((far, cols), BF16)] * 2 + [struct(known.shape, F32)],
    )(qs, gs, mine, theirs, known)


def remote_body(depth, scale, width, qs, gs, inner, outer, far_k, far_v, known, *rest):
    far_kt, near_t, near_d, s_held, d_held = rest[6:]
    rows = qs.shape[1]
    blocks = rows // BLOCK
    half = far_k.shape[0] // 2
    heads = qs.shape[0]
    pair = pl.program_id(0)
    lanes = pl.ds(pl.multiple_of(pair * width, width), width)
    far_k, far_v = (ref.at[:, lanes] for ref in (far_k, far_v))
    qs, gs, inner, outer = (ref.at[:, :, lanes] for ref in (qs, gs, inner, outer))
    kept, sent, inner_d, outer_d = (ref.at[:, :, lanes] for ref in rest[:4])
    dq_t = rest[4].at[lanes]
    final = rest[5].at[pair]
    known = known.at[pair]
    far_kt[...] = (far_k[...].astype(F32) * scale).astype(BF16).T
    near_t[0] = (inner[0].astype(F32) * scale).astype(BF16).T
    near_t[1] = (outer[0].astype(F32) * scale).astype(BF16).T
    odd = is_odd()
    position = lax.axis_index("seq")
    ends = (position == 0) | (position == lax.axis_size("seq") - 1)
    missing = jnp.where(ends, NEG, 0.0)
    places = [
        pl.ds(pl.multiple_of(n * ((blocks - 1) * BLOCK), BLOCK), BLOCK) for n in (1 - odd, odd)
    ]
    halos = ((inner, None), (outer, missing))
    final[0] = known[0] + jnp.log(known[1])
    final[1] = known[2] / known[1]
    for h in range(heads):
        old = None
        for n, ((halo, bias), r) in enumerate(zip(halos, places)):
            if old is None or blocks > 1:
                old = [known[m, h : h + 1, r] for m in range(3)]
            s = dot(halo[0], qs[h, r], NT)
            if bias is not None:
                s = s + bias
            d = dot(halo[1], gs[h, r], NT)
            s_held[2 * h + n] = s
            d_held[2 * h + n] = d
            old = settle(old, merge(None, s, d))
            final[0, h : h + 1, r] = old[0] + jnp.log(old[1])
            final[1, h : h + 1, r] = old[2] / old[1]
    totals = [None, None]
    for h in range(heads):
        hr = slice(h * depth, (h + 1) * depth)
        p = jnp.exp(dot(far_k[...], qs[h], NT) - final[0, h : h + 1, :])
        ds = (p * (dot(far_v[...], gs[h], NT) - final[1, h : h + 1, :])).astype(BF16)
        parts = (dot(ds, qs[h], NN), dot(p.astype(BF16), gs[h], NN))
        totals = [new if old is None else old + new for old, new in zip(totals, parts)]
        dq_t[hr] = dot(far_kt[hr], ds, NN)
        for n, r in enumerate(places):
            p = jnp.exp(s_held[2 * h + n] - final[0, h : h + 1, r])
            ds = (p * (d_held[2 * h + n] - final[1, h : h + 1, r])).astype(BF16)
            parts = (dot(ds, qs[h, r], NN), dot(p.astype(BF16), gs[h, r], NN))
            for m, part in enumerate(parts):
                if h == 0:
                    near_d[2 * n + m] = part
                else:
                    near_d[2 * n + m] += part
            dq_t[hr, r] += dot(near_t[n, hr], ds, NN)
    for n in range(2):
        kept[n] = totals[n][:half]
        sent[n] = totals[n][half:].astype(BF16)
        inner_d[n] = near_d[n].astype(BF16)
        outer_d[n] = near_d[2 + n].astype(BF16)


def remote(qs, gs, inner, outer, far_k, far_v, known, width, depth, scale):
    rows, cols = qs.shape[1:]
    pairs = cols // width
    hp = width // depth
    far = far_k.shape[0]
    half = far // 2
    return call(
        functools.partial(remote_body, depth, scale, width),
        flops=10 * (far * rows + 2 * BLOCK * BLOCK) * cols,
        moved=rows * cols * 8,
        grid=(pairs,),
        in_specs=[WHOLE] * 7,
        out_specs=[WHOLE] * 6,
        scratch_shapes=[
            pltpu.VMEM((width, far), BF16),
            pltpu.VMEM((2, width, BLOCK), BF16),
            pltpu.VMEM((4, BLOCK, width), F32),
            pltpu.VMEM((2 * hp, BLOCK, BLOCK), F32),
            pltpu.VMEM((2 * hp, BLOCK, BLOCK), F32),
        ],
        out_shape=[
            struct((2, half, cols), F32),
            struct((2, half, cols), BF16),
            struct((2, BLOCK, cols), BF16),
            struct((2, BLOCK, cols), BF16),
            struct((cols, rows), F32),
            struct((pairs, 2, hp, rows), F32),
        ],
    )(qs, gs, inner, outer, far_k, far_v, known)


def local_body(depth, scale, width, pair, chained, *refs):
    lanes = slice(pair * width, (pair + 1) * width)
    q, k, v, g = (ref.at[:, lanes] for ref in refs[:4])
    part = refs[4].at[lanes]
    final = refs[5].at[pair]
    dq, dk, dv, *rest = refs[6 + chained :]
    k_t, dq_t = rest[chained > 0 :][:2]
    if chained:
        earlier = slice((pair - 1) * width, pair * width)
        copy = pltpu.make_async_copy(refs[6], rest[0].at[:, earlier], rest[3])
        copy.start()
    rows = q.shape[0]
    blocks = rows // BLOCK
    k_t[...] = (k[...].astype(F32) * scale).astype(BF16).T
    for h, mask in enumerate(head_masks(width, depth)):
        hr = slice(h * depth, (h + 1) * depth)
        for b in range(blocks):
            r = slice(b * BLOCK, (b + 1) * BLOCK)
            qs = keep_head(q[r], mask, scale)
            gs = keep_head(g[r], mask)
            reach = near(b, blocks)
            c = slice(reach[0] * BLOCK, (reach[-1] + 1) * BLOCK)
            p = jnp.exp(dot(k[c], qs, NT) - final[0, h : h + 1, r])
            ds = (p * (dot(v[c], gs, NT) - final[1, h : h + 1, r])).astype(BF16)
            v_part = dot(p.astype(BF16), gs, NN)
            k_part = dot(ds, qs, NN)
            for n, j in enumerate(reach):
                rj = slice(j * BLOCK, (j + 1) * BLOCK)
                here = slice(n * BLOCK, (n + 1) * BLOCK)
                if h == 0 and b == near(j, blocks)[0]:
                    dv[rj] = v_part[here]
                    dk[rj] = k_part[here]
                else:
                    dv[rj] += v_part[here]
                    dk[rj] += k_part[here]
            dq_t[hr, r] = part[hr, r] + dot(k_t[hr, c], ds, NN)
    dq[...] = dq_t[...].T.astype(BF16)
    if chained:
        copy.wait()


def local(q, k, v, g, part, final, earlier, width, depth, scale, pair):
    rows, cols = q.shape
    chained = len(earlier)
    tile, wide = struct((rows, width), BF16), struct((rows, width), F32)
    return call(
        functools.partial(local_body, depth, scale, width, pair, chained),
        flops=10 * 3 * BLOCK * rows * width,
        moved=rows * width * 24,
        in_specs=[WHOLE] * 6 + [WHOLE, ANY][:chained],
        out_specs=[WHOLE] * 3 + [HBM] * (chained > 0),
        out_shape=[tile, wide, wide] + [struct((rows, cols), BF16)] * (chained > 0),
        scratch_shapes=[pltpu.VMEM((width, rows), BF16), pltpu.VMEM((width, rows), F32)]
        + [pltpu.SemaphoreType.DMA] * (chained > 0),
        input_output_aliases={7: 3} if chained == 2 else {},
    )(q, k, v, g, part, final, *earlier)


def gathered(kept, got, n):
    rows = kept.shape[1]
    total = kept[n]
    for part in got:
        at = rows - part.shape[1]
        more = part[n].astype(F32)
        if at:
            more = jnp.concatenate([jnp.zeros((at, more.shape[1]), F32), more], axis=0)
        total = total + more
    return total


def fold(kept, got, cuts, tokens=(), passed=()):
    cols = kept.shape[-1]
    vmem = pl.BlockSpec(memory_space=pltpu.VMEM)
    extra = list(passed) + list(tokens)
    count = len(got)
    sizes = [b - a for a, b in zip(cuts, cuts[1:])]

    def body(kept, *rest):
        arrived = rest[:count]
        outs = rest[count + len(extra) :]
        for n in range(2):
            total = gathered(kept, arrived, n)
            outs[0][n] = total[: cuts[0]]
            for a, b, out in zip(cuts, cuts[1:], outs[1:]):
                out[n] = total[a:b].astype(BF16)

    return call(
        body,
        moved=kept.size * 8,
        in_specs=[vmem] * (1 + count) + [ANY] * len(extra),
        out_specs=[vmem] * len(cuts) + [ANY] * len(passed),
        out_shape=[struct((2, cuts[0], cols), F32)]
        + [struct((2, size, cols), BF16) for size in sizes]
        + [struct(x.shape, x.dtype) for x in passed],
        input_output_aliases={1 + count + n: len(cuts) + n for n in range(len(passed))},
    )(kept, *got, *extra)


def finish_body(pairs, depth, count, *refs):
    dk, dv = refs[:pairs], refs[pairs : 2 * pairs]
    from_inner, from_outer, group_pool, whole_pool, kept = refs[2 * pairs : 2 * pairs + 5]
    got = refs[2 * pairs + 5 : 2 * pairs + 5 + count]
    tile = refs[2 * pairs + 5 + count]
    out_k, out_v, out_q, left, total, sem = refs[-6:]
    block = pl.program_id(0)
    last = slice((pairs - 1) * tile.shape[1], pairs * tile.shape[1])
    copy = pltpu.make_async_copy(tile, out_q.at[:, last], sem)
    pl.when(block == 0)(copy.start)
    rows, cols = kept.shape[1:]
    heads = group_pool.shape[0]
    width = dk[0].shape[1]
    per = BLOCK // SEG1
    count1 = rows * SEG2 // (SEG1 + SEG2)
    blocks = count1 // per

    @pl.when(block == 0)
    def _():
        a, b, c = (t.astype(F32) for t in split(pooling(group_pool[...], whole_pool[...])))
        left[...] = jnp.concatenate([a, a, a, b, b, c], axis=0).T.astype(BF16)
        for n in range(2):
            total[n] = gathered(kept, got, n)

    def emit(halos):
        pick = head_columns(heads, cols, depth)
        for n, (src, dst) in enumerate(((dk, out_k), (dv, out_v))):
            places = [block * per + s for s in range(per)] + [count1 + block]
            found = [jnp.where(pick, total[n, pl.ds(at, 1)], 0.0) for at in places]
            a, b, c = split(jnp.concatenate(found, axis=0))
            spread = dot(left[...], jnp.concatenate([a, b, c, a, b, a], axis=0), NN)
            for halo in halos:
                spread = spread + halo[n].astype(F32)
            for p in range(pairs):
                lanes = slice(p * width, (p + 1) * width)
                dst[:, lanes] = (spread[:, lanes] + src[p][...]).astype(BF16)

    if blocks == 1:
        emit((from_inner, from_outer))
        copy.wait()
        return
    odd = is_odd()
    at_inner = block == (1 - odd) * (blocks - 1)
    at_outer = block == odd * (blocks - 1)
    pl.when(at_inner)(lambda: emit((from_inner,)))
    pl.when(at_outer)(lambda: emit((from_outer,)))
    pl.when(jnp.logical_not(at_inner | at_outer))(lambda: emit(()))
    pl.when(block == blocks - 1)(copy.wait)


def finish(dk, dv, from_inner, from_outer, kept, got, group_pool, whole_pool, earlier):
    rows, width = dk[0].shape
    pairs = len(dk)
    cols = width * pairs
    depth = cols // group_pool.shape[0]
    out = pl.BlockSpec((BLOCK, cols), lambda i: (i, 0))
    narrow = pl.BlockSpec((BLOCK, width), lambda i: (i, 0))
    fixed = [from_inner, from_outer, group_pool, whole_pool, kept] + list(got)
    place = 2 * pairs + len(fixed) + 1
    return call(
        functools.partial(finish_body, pairs, depth, len(got)),
        moved=rows * cols * 12,
        grid=(rows // BLOCK,),
        in_specs=[narrow] * (2 * pairs)
        + [WHOLE] * (len(fixed) + 1)
        + [ANY] * (len(earlier) - 1),
        out_specs=[out, out, HBM],
        out_shape=[struct((rows, cols), BF16)] * 3,
        scratch_shapes=[
            pltpu.VMEM((SEG2, 6 * (BLOCK // SEG1 + 1) * group_pool.shape[0]), BF16),
            pltpu.VMEM(kept.shape, F32),
            pltpu.SemaphoreType.DMA,
        ],
        input_output_aliases={place: 2} if len(earlier) == 2 else {},
    )(*dk, *dv, *fixed, *earlier)


def shards(query, key, value, out_grad, pool_group, pool_global):
    rows, cols = query.shape
    heads = pool_group.shape[0]
    depth = cols // heads
    scale = 1.0 / math.sqrt(depth)
    width = 128 if cols % 128 == 0 and 128 % depth == 0 else cols
    pairs = cols // width
    devices = lax.axis_size("seq")
    count1 = rows // SEG1
    group_bits = list(range(1, GROUP.bit_length() - 1))
    other_bits = list(range(GROUP.bit_length() - 1, devices.bit_length() - 1))

    def swap(array, *bits):
        mask = sum(1 << bit for bit in bits)
        return lax.ppermute(array, "seq", [(i, i ^ mask) for i in range(devices)])

    def cross(array):
        route = [(i, i + 1) for i in range(1, devices - 1, 2)]
        return lax.ppermute(array, "seq", route + [(b, a) for a, b in route])

    groups, wholes, inner, outer, key, value = pool(key, value, pool_group, pool_global)
    partial = [
        stats(query, key, value, out_grad, width, depth, scale, p) for p in range(pairs)
    ]
    waiting = list(partial)

    def token():
        return [waiting.pop(0)] if waiting else []

    for bit in other_bits[:-1]:
        got = swap(wholes, bit)
        wholes = join([[wholes, got]])[0][0]
    base, far_bit = group_bits[0], other_bits[-1:]
    (pair,) = join([[groups, wholes]])
    here, there = [groups, wholes], []
    there = [swap(pair[0], base)]
    for bit in far_bit:
        here.append(swap(wholes, bit))
        there.append(swap(wholes, base, bit))
    comb, inner = join([here, there], token(), [inner])
    for bit in group_bits[1:]:
        got = swap(comb, bit)
        (comb,) = join([comb, got], token() + token() + token())
    theirs = swap(comb, 0)
    outer = cross(outer)
    inner = swap(inner, 0)

    qs, gs, known = far_stats(query, out_grad, comb, partial, width, depth, scale)
    far_k, far_v, known = more_stats(qs, gs, comb, theirs, known, width)
    kept, sent, inner_d, outer_d, dq_t, final = remote(
        qs, gs, inner, outer, far_k, far_v, known, width, depth, scale
    )
    got = [swap(sent, 0)]

    earlier, dk, dv = [], [], []

    def step():
        nonlocal earlier
        if len(dk) == pairs:
            return []
        tile, a, b, *rest = local(
            query, key, value, out_grad, dq_t, final, earlier, width, depth, scale, len(dk)
        )
        earlier = [tile] + rest
        dk.append(a)
        dv.append(b)
        return [a]

    from_inner = from_outer = None
    for bit in reversed(group_bits[1:]):
        size = kept.shape[1]
        if from_outer is None:
            kept, sent, inner_d, outer_d = fold(
                kept, got, [size // 2, size], step(), [inner_d, outer_d]
            )
            got = [swap(sent, bit)]
            from_outer = cross(outer_d)
            from_inner = swap(inner_d, 0)
        else:
            kept, sent = fold(kept, got, [size // 2, size], step())
            got = [swap(sent, bit)]
    slot = kept.shape[1] // 2
    own = slot - (slot - count1) // 2 if far_bit else slot
    last = []
    while len(dk) < pairs - 1:
        last = step()
    if far_bit:
        kept, far_here, to_base, far_there = fold(kept, got, [own, slot, slot + own, 2 * slot], last)
        got = [swap(to_base, base), swap(far_here, far_bit[0]), swap(far_there, base, far_bit[0])]
    else:
        kept, to_base = fold(kept, got, [slot, 2 * slot], last)
        got = [swap(to_base, base)]
    for bit in reversed(other_bits[:-1]):
        size = kept.shape[1]
        cut = count1 + (size - count1) // 2
        kept, sent = fold(kept, got, [cut, size])
        got = [swap(sent, bit)]
    while len(dk) < pairs:
        step()
    key_grad, value_grad, query_grad = finish(
        dk, dv, from_inner, from_outer, kept, got, pool_group, pool_global, earlier
    )
    return (query_grad, key_grad, value_grad)


def solution(mesh):
    rows = P("seq", "head")
    in_specs = (rows, rows, rows, rows, P("head", None), P("head", None))
    return jax.shard_map(
        shards, mesh=mesh, in_specs=in_specs, out_specs=(rows, rows, rows), check_vma=False
    )
```
